32 devices in a mesh: grp: 2 (over core), blk: 16 (over z, y, x).
Axes of the slice: x: 2, y: 2, z: 4, core: 2. Of those that a mesh axis runs over, the one named last changes fastest.
Arguments:
- src_feats: bfloat16 [2, 4096, 512], P('grp', 'blk')
- tgt_feats: bfloat16 [2, 4096, 512], P('grp', 'blk')
- proj_weight: bfloat16 [512, 512], replicated, may hold values from -0.25 to 0.25
- match_blocks: int32 [2, 32, 4], P('grp', 'blk'), may hold values from 0 to 31, as said below
- match_count: int32 [2, 32], P('grp', 'blk'), may hold values from 1 to 4
- pair_src: int32 [2, 32, 4, 128], P('grp', 'blk'), may hold values from 0 to 127
- pair_tgt: int32 [2, 32, 4, 128], P('grp', 'blk'), may hold values from 0 to 127
Outputs:
- weight_grad: float32 [512, 512], replicated
- covariance: float32 [2, 512, 512], P('grp')
The draws below stay inside these ranges and needn't reach their ends.
Inputs may be any that keep to these rules, and one draw needn't show every extreme that they name: `match_blocks`: each row lists 4 different target blocks; for source block s each listed block t has t // 2 at most 1 away from s // 2 along the loop of 16 runs (taken mod 16); unused slots follow the same rule.
All inputs are finite; a program needn't handle non-finite values.
Results may differ from the reference program's by a relative error of at most 0.0052.
Values may be sent and summed in bfloat16 or wider, within the bound.
No kernel may reach another device: no remote copies, remote signals or barrier semaphores. Data moves between devices by JAX's collectives and lax.ppermute only.
A program may use at most 64 MiB of HBM per device.

```python
import math
import jax
import jax.numpy as jnp
from jax import lax

D = 512
PB = 128
BPD = 2
LMAX = 4
MP = 128
REACH = 1
NBLOCKS = 32
NPTS = 4096
N_GRP = 2
N_BLK = 16


def feature_draw(key, salt_value):
    key_scale, key_base = jax.random.split(jax.random.fold_in(key, salt_value), 2)
    scales = jnp.exp(jax.random.uniform(key_scale, (N_GRP, NBLOCKS, 1, D), minval=0.0, maxval=math.log(10.0)))
    values_out = jax.random.normal(key_base, (N_GRP, NBLOCKS, PB, D)) * scales
    return values_out.astype(jnp.float32).reshape(N_GRP, NPTS, D).astype(jnp.bfloat16)


def draw_src_feats(key, part):
    return feature_draw(key, 11)


def draw_tgt_feats(key, part):
    return feature_draw(key, 13)


def draw_match_blocks(key, part):
    window = (2 * REACH + 1) * BPD
    scores = jax.random.randint(jax.random.fold_in(key, 3), (N_GRP, NBLOCKS, window), 0, 1 << 20)
    scores = scores * window + jnp.arange(window, dtype=jnp.int32)
    ranked = jnp.argsort(scores, axis=-1, stable=True)[..., :LMAX].astype(jnp.int32)
    run_offset = ranked // BPD - REACH
    nested_block = ranked % BPD
    owning_run_index = (jnp.arange(NBLOCKS, dtype=jnp.int32) // BPD)[None, :, None]
    return ((owning_run_index + run_offset) % N_BLK * BPD + nested_block).astype(jnp.int32)


def draw_match_count(key, part):
    factor_one = jax.random.randint(jax.random.fold_in(key, 5), (N_GRP, NBLOCKS), 0, LMAX)
    factor_two = jax.random.randint(jax.random.fold_in(key, 7), (N_GRP, NBLOCKS), 0, LMAX + 1)
    block_count = 1 + factor_one * factor_two // LMAX
    position = jnp.arange(NBLOCKS, dtype=jnp.int32)[None, :]
    block_count = jnp.where(position == 0, LMAX, block_count)
    block_count = jnp.where(position == 1, 1, block_count)
    return block_count.astype(jnp.int32)


def touch_ends(entries, rng, least, high):
    longest = entries.shape.index(max(entries.shape))
    spots = []
    for shift in (0, 1):
        where = [jax.random.randint(jax.random.fold_in(rng, axis), (), 0, length) for axis, length in enumerate(entries.shape)]
        where[longest] = (where[longest] + shift) % entries.shape[longest]
        spots.append(tuple(where))
    return entries.at[spots[0]].set(least).at[spots[1]].set(high)


def bell_draw(rng, shape, spread, most, kind=jnp.bfloat16):
    drawn = spread * jax.random.normal(rng, shape, jnp.float32)
    return jnp.clip(drawn, min=-most, max=most).astype(kind)


def setup_inputs(seed: int = 0) -> dict:
    key_list = jax.random.split(jax.random.key(seed), 8)
    return {
        "src_feats": draw_src_feats(jax.random.fold_in(key_list[7], 71), 0),
        "tgt_feats": draw_tgt_feats(jax.random.fold_in(key_list[7], 71), 0),
        "proj_weight": bell_draw(key_list[2], (D, D), D ** -0.5, 0.25),
        "match_blocks": draw_match_blocks(jax.random.fold_in(key_list[7], 71), 0),
        "match_count": draw_match_count(jax.random.fold_in(key_list[7], 71), 0),
        "pair_src": touch_ends(jax.random.randint(key_list[5], (N_GRP, NBLOCKS, LMAX, MP), 0, PB), jax.random.fold_in(key_list[5], 1), 0, PB - 1).astype(jnp.int32),
        "pair_tgt": touch_ends(jax.random.randint(key_list[6], (N_GRP, NBLOCKS, LMAX, MP), 0, PB), jax.random.fold_in(key_list[6], 1), 0, PB - 1).astype(jnp.int32),
    }


sharpness_divisor = 0.4
logit_bound = 2.5
norm_eps = 1e-06

def project(features, weight_mat):
    projected = jnp.dot(features, weight_mat, preferred_element_type=jnp.float32)
    inv_norm = lax.rsqrt(lax.optimization_barrier(jnp.sum(projected * projected, axis=1, keepdims=True)) + norm_eps)
    unit_rows = projected * inv_norm
    return (unit_rows, inv_norm, unit_rows.astype(jnp.bfloat16))

def back_norm(unit_rows, inv_norm, grad_rows):
    inner = lax.optimization_barrier(jnp.sum(unit_rows * grad_rows, axis=1, keepdims=True))
    return ((grad_rows - unit_rows * inner) * inv_norm).astype(jnp.bfloat16)

def reference(src_feats, tgt_feats, proj_weight, match_blocks, match_count, pair_src, pair_tgt):

    def group_step(group_index):
        src_rows = src_feats[group_index]
        tgt_rows = tgt_feats[group_index]
        src_unit, source_inverse_norm, src_half = project(src_rows, proj_weight)
        tgt_unit, tgt_inv, tgt_half = project(tgt_rows, proj_weight)
        src_blocks = src_half.reshape(NBLOCKS, PB, D)
        tgt_blocks = tgt_half.reshape(NBLOCKS, PB, D)
        listed_all = match_blocks[group_index]
        counts_all = match_count[group_index]
        sources_all = pair_src[group_index]
        targets_all = pair_tgt[group_index]
        columns = jnp.arange(PB, dtype=jnp.int32)
        slot_index = jnp.arange(LMAX, dtype=jnp.int32)

        def score_block(accum, block_id):
            listed = listed_all[block_id]
            live_slots = (slot_index < counts_all[block_id]).astype(jnp.float32)
            sources = sources_all[block_id]
            targets = targets_all[block_id]
            anchor_embeddings = src_blocks[block_id][sources].astype(jnp.float32)
            candidate_embeddings = tgt_blocks[listed].astype(jnp.float32)
            similarity_table = jnp.einsum('tku,tiu->tki', anchor_embeddings, candidate_embeddings) / sharpness_divisor
            exp_terms = jnp.exp(similarity_table - logit_bound)
            shares = exp_terms / lax.optimization_barrier(jnp.sum(exp_terms, axis=2, keepdims=True))
            onehot = (targets[:, :, None] == columns[None, None, :]).astype(jnp.float32)
            linear_map_coefficients = ((shares - onehot) * live_slots[:, None, None]).astype(jnp.bfloat16).astype(jnp.float32)
            anchor_loss_slope = jnp.einsum('qtk,qkc->qtc', linear_map_coefficients, candidate_embeddings) / sharpness_divisor
            candidate_loss_slopes = jnp.einsum('xhw,xhe->xwe', linear_map_coefficients, anchor_embeddings) / sharpness_divisor
            accum = accum.at[listed].add(candidate_loss_slopes)
            grad_source = jax.ops.segment_sum(anchor_loss_slope.reshape(LMAX * MP, D), sources.reshape(LMAX * MP), num_segments=PB)
            return (accum, grad_source)
        grad_tgt, grad_src = lax.scan(score_block, jnp.zeros((NBLOCKS, PB, D), jnp.float32), jnp.arange(NBLOCKS, dtype=jnp.int32))
        src_grad = back_norm(src_unit, source_inverse_norm, grad_src.reshape(NPTS, D))
        tgt_grad = back_norm(tgt_unit, tgt_inv, grad_tgt.reshape(NPTS, D))
        weight_part = jnp.dot(src_rows.T, src_grad, preferred_element_type=jnp.float32) + jnp.dot(tgt_rows.T, tgt_grad, preferred_element_type=jnp.float32)
        moment = jnp.dot(src_half.T, src_half, preferred_element_type=jnp.float32) + jnp.dot(tgt_half.T, tgt_half, preferred_element_type=jnp.float32)
        return (weight_part, moment * (D / (2.0 * NPTS)))
    weight_parts, covariance = lax.map(group_step, jnp.arange(N_GRP, dtype=jnp.int32))
    return (lax.optimization_barrier(jnp.sum(weight_parts, axis=0)), covariance)
```

```python
import functools
import jax
import jax.numpy as jnp
from jax import lax
from jax.experimental import pallas as pl
from jax.experimental.pallas import tpu as pltpu
from jax.sharding import PartitionSpec as P

inverse_sharpness = 2.5
logit_bound = 2.5
norm_eps = 1e-06
lane = 128

f32 = jnp.float32
bf16 = jnp.bfloat16


def dot_nn(a, b):
    return lax.dot_general(a, b, (((1,), (0,)), ((), ())), preferred_element_type=f32)


def dot_nt(a, b):
    return lax.dot_general(a, b, (((1,), (1,)), ((), ())), preferred_element_type=f32)


def dot_tn(a, b):
    return lax.dot_general(a, b, (((0,), (0,)), ((), ())), preferred_element_type=f32)


def project(rows, weight):
    projected = dot_nn(rows, weight)
    inv_norm = lax.rsqrt(jnp.sum(projected * projected, axis=1, keepdims=True) + norm_eps)
    return projected * inv_norm, inv_norm


def back_norm(unit, inv_norm, grad):
    inner = jnp.sum(unit * grad, axis=1, keepdims=True)
    return ((grad - unit * inner) * inv_norm).astype(bf16)


def pair_weights(anchors, candidates, counts, block):
    logits = dot_nt(anchors, candidates)
    terms = jnp.exp(logits * inverse_sharpness - logit_bound)
    parts = []
    for first in range(0, candidates.shape[0], block):
        part = terms[:, first : first + block]
        count = counts[:, first : first + block].astype(f32)
        pairs = jnp.sum(count, axis=1, keepdims=True)
        total = jnp.sum(part, axis=1, keepdims=True)
        parts.append((part * (pairs / total) - count).astype(bf16))
    return jnp.concatenate(parts, axis=1)


def pair_counts(src_ref, key_ref, blocks, slots, block, candidates):
    pairs = src_ref.shape[1]
    point = lax.broadcasted_iota(jnp.int32, (block, pairs), 0)
    place = lax.broadcasted_iota(jnp.int32, (candidates * block, pairs), 0)
    rows = []
    for b in range(blocks):
        left = []
        right = []
        for s in range(b * slots, (b + 1) * slots):
            left.append(jnp.where(src_ref[s : s + 1, :] == point, 1.0, 0.0).astype(bf16))
            right.append(jnp.where(key_ref[s : s + 1, :] == place, 1.0, 0.0).astype(bf16))
        rows.append(dot_nt(jnp.concatenate(left, axis=1), jnp.concatenate(right, axis=1)))
    return jnp.concatenate(rows, axis=0)


def own_kernel(
    blocks, slots, block, candidates, scale,
    xs_ref, xt_ref, w_ref, src_ref, key_ref,
    moment_ref, unit_ref, inv_ref, count_ref, grad_ref, part_ref,
):
    weight = w_ref[...]
    src_unit, src_inv = project(xs_ref[...], weight)
    tgt_unit, tgt_inv = project(xt_ref[...], weight)
    zs = src_unit.astype(bf16)
    zt = tgt_unit.astype(bf16)
    unit_ref[...] = src_unit
    inv_ref[...] = jnp.broadcast_to(src_inv, inv_ref.shape)
    moment = (dot_tn(zs, zs) + dot_tn(zt, zt)) * scale
    at = 0
    for r in range(0, moment.shape[0], lane):
        for c in range(r, moment.shape[1], lane):
            moment_ref[at : at + lane, :] = moment[r : r + lane, c : c + lane].astype(bf16)
            at += lane
    counts = pair_counts(src_ref, key_ref, blocks, slots, block, candidates)
    own = blocks * block
    count_ref[...] = counts[:, own:].astype(bf16)
    weights = pair_weights(zs, zt, counts[:, :own], block)
    grad_ref[...] = dot_nn(weights, zt)
    grad_zt = dot_tn(weights, zs) * inverse_sharpness
    part_ref[...] = dot_tn(xt_ref[...], back_norm(tgt_unit, tgt_inv, grad_zt))


def halo_kernel(
    nbrs, block, groups,
    grp_ref, xs_ref, w_ref, unit_ref, inv_ref, count_ref, grad_ref, part_ref, *refs,
):
    nbr_refs = refs[:nbrs]
    keep_ref, send_ref, total_ref = refs[nbrs:]
    weight = w_ref[...]
    rows = jnp.concatenate([r[...] for r in nbr_refs], axis=0)
    tgt_unit, tgt_inv = project(rows, weight)
    zt = tgt_unit.astype(bf16)
    src_unit = unit_ref[...]
    zs = src_unit.astype(bf16)
    weights = pair_weights(zs, zt, count_ref[...], block)
    grad_zs = (grad_ref[...] + dot_nn(weights, zt)) * inverse_sharpness
    grad_zt = dot_tn(weights, zs) * inverse_sharpness
    src_grad = back_norm(src_unit, inv_ref[:, :1], grad_zs)
    tgt_grad = back_norm(tgt_unit, tgt_inv, grad_zt)
    total_ref[...] = part_ref[...] + dot_tn(xs_ref[...], src_grad) + dot_tn(rows, tgt_grad)
    chunk = total_ref.shape[0] // groups
    me = grp_ref[0]
    keep_ref[...] = total_ref[pl.ds(pl.multiple_of(me * chunk, chunk), chunk), :]
    for k in range(1, groups):
        first = lax.rem(me + k, groups) * chunk
        send_ref[k - 1] = total_ref[pl.ds(pl.multiple_of(first, chunk), chunk), :].astype(bf16)


def unpack_kernel(packed_ref, out_ref):
    at = 0
    for r in range(0, out_ref.shape[0], lane):
        for c in range(r, out_ref.shape[1], lane):
            tile = packed_ref[at : at + lane, :].astype(f32)
            out_ref[r : r + lane, c : c + lane] = tile
            if c > r:
                out_ref[c : c + lane, r : r + lane] = tile.T
            at += lane


def body(src_feats, tgt_feats, proj_weight, match_blocks, match_count, pair_src, pair_tgt):
    xs = src_feats[0]
    xt = tgt_feats[0]
    points, width = xs.shape
    blocks, slots, pairs = pair_src.shape[1:]
    block = points // blocks
    runs = lax.axis_size("blk")
    groups = lax.axis_size("grp")
    reach = runs // 16
    run = lax.axis_index("blk")
    grp = lax.axis_index("grp")

    nbrs = []
    for k in range(1, reach + 1):
        nbrs.append(lax.ppermute(xt, "blk", [(i, (i - k) % runs) for i in range(runs)]))
        nbrs.append(lax.ppermute(xt, "blk", [(i, (i + k) % runs) for i in range(runs)]))

    listed = match_blocks[0]
    offset = (listed // blocks - run + reach) % runs - reach
    order = jnp.where(offset > 0, 2 * offset - 1, -2 * offset)
    live = jnp.arange(slots, dtype=jnp.int32)[None, :] < match_count[0][:, None]
    first = (order * blocks + listed % blocks) * block
    keys = jnp.where(live[:, :, None], first[:, :, None] + pair_tgt[0], -1)
    keys = keys.reshape(blocks * slots, pairs)
    sources = pair_src[0].reshape(blocks * slots, pairs)

    candidates = (2 * reach + 1) * blocks
    tiles = width // lane
    packed_rows = tiles * (tiles + 1) // 2 * lane
    chunk = width // groups
    scale = width / (2.0 * points * runs)
    vmem = pl.BlockSpec(memory_space=pltpu.VMEM)
    smem = pl.BlockSpec(memory_space=pltpu.SMEM)

    packed, unit, inv, counts, grad, part = pl.pallas_call(
        functools.partial(own_kernel, blocks, slots, block, candidates, scale),
        out_shape=(
            jax.ShapeDtypeStruct((packed_rows, lane), bf16),
            jax.ShapeDtypeStruct((points, width), f32),
            jax.ShapeDtypeStruct((points, lane), f32),
            jax.ShapeDtypeStruct((points, (candidates - blocks) * block), bf16),
            jax.ShapeDtypeStruct((points, width), f32),
            jax.ShapeDtypeStruct((width, width), f32),
        ),
        in_specs=[vmem] * 5,
        out_specs=(vmem,) * 6,
        name="own",
    )(xs, xt, proj_weight, sources, keys)

    moved = lax.all_to_all(packed.reshape(runs, packed_rows // runs, lane), "blk", 0, 0)
    keep, send = pl.pallas_call(
        functools.partial(halo_kernel, 2 * reach, block, groups),
        out_shape=(
            jax.ShapeDtypeStruct((chunk, width), f32),
            jax.ShapeDtypeStruct((groups - 1, chunk, width), bf16),
        ),
        in_specs=[smem] + [vmem] * (7 + 2 * reach),
        out_specs=(vmem, vmem),
        scratch_shapes=[pltpu.VMEM((width, width), f32)],
        name="halo",
    )(grp.reshape(1), xs, proj_weight, unit, inv, counts, grad, part, *nbrs)

    total = keep
    for k in range(1, groups):
        got = lax.ppermute(send[k - 1], "grp", [(i, (i + k) % groups) for i in range(groups)])
        total = total + got.astype(f32)
    piece = chunk // runs
    spread = lax.all_to_all(total.astype(bf16).reshape(runs, piece, width), "blk", 0, 0)
    mine = jnp.sum(spread.astype(f32), axis=0).astype(bf16)
    whole = lax.all_to_all(jnp.broadcast_to(mine, (runs, piece, width)), "blk", 0, 0)
    half = whole.reshape(chunk, width)
    parts = [half]
    for k in range(1, groups):
        parts.append(lax.ppermute(half, "grp", [(i, (i - k) % groups) for i in range(groups)]))
    if groups == 2:
        low = jnp.where(grp == 0, parts[0], parts[1])
        high = jnp.where(grp == 0, parts[1], parts[0])
        weight_grad = jnp.concatenate([low, high], axis=0).astype(f32)
    else:
        stacked = jnp.stack(parts)
        place = (jnp.arange(groups, dtype=jnp.int32) - grp) % groups
        weight_grad = jnp.take(stacked, place, axis=0).reshape(width, width).astype(f32)

    mine_c = jnp.sum(moved.astype(f32), axis=0).astype(bf16)
    packed_all = lax.all_to_all(
        jnp.broadcast_to(mine_c, (runs, packed_rows // runs, lane)), "blk", 0, 0
    )
    covariance = pl.pallas_call(
        unpack_kernel,
        out_shape=jax.ShapeDtypeStruct((width, width), f32),
        in_specs=[vmem],
        out_specs=vmem,
        name="unpack",
    )(packed_all.reshape(packed_rows, lane))
    return (weight_grad, covariance[None])


def solution(mesh):
    placed = (
        P("grp", "blk", None),
        P("grp", "blk", None),
        P(),
        P("grp", "blk", None),
        P("grp", "blk"),
        P("grp", "blk", None, None),
        P("grp", "blk", None, None),
    )
    return jax.shard_map(
        body, mesh=mesh, in_specs=placed, out_specs=(P(), P("grp", None, None)), check_vma=False
    )
```

```python
import functools
import jax
import jax.numpy as jnp
from jax import lax
from jax.experimental import pallas as pl
from jax.experimental.pallas import tpu as pltpu
from jax.sharding import PartitionSpec as P


inverse_sharpness = 2.5
logit_bound = 2.5
norm_eps = 1e-06
lane = 128

f32 = jnp.float32
bf16 = jnp.bfloat16


def dot_nn(a, b):
    return lax.dot_general(a, b, (((1,), (0,)), ((), ())), preferred_element_type=f32)


def dot_nt(a, b):
    return lax.dot_general(a, b, (((1,), (1,)), ((), ())), preferred_element_type=f32)


def dot_tn(a, b):
    return lax.dot_general(a, b, (((0,), (0,)), ((), ())), preferred_element_type=f32)


def room(mebibytes):
    return pltpu.CompilerParams(vmem_limit_bytes=mebibytes * 1024 * 1024)


def project(rows, weight):
    projected = dot_nn(rows, weight)
    inv_norm = lax.rsqrt(jnp.sum(projected * projected, axis=1, keepdims=True) + norm_eps)
    return projected * inv_norm, inv_norm


def back_norm(unit, inv_norm, grad):
    inner = jnp.sum(unit * grad, axis=1, keepdims=True)
    return ((grad - unit * inner) * inv_norm).astype(bf16)


def pair_weights(anchors, candidates, counts, block):
    logits = dot_nt(anchors, candidates)
    terms = jnp.exp(logits * inverse_sharpness - logit_bound)
    parts = []
    for first in range(0, candidates.shape[0], block):
        part = terms[:, first : first + block]
        count = counts[:, first : first + block].astype(f32)
        pairs = jnp.sum(count, axis=1, keepdims=True)
        total = jnp.sum(part, axis=1, keepdims=True)
        parts.append((part * (pairs / total) - count).astype(bf16))
    return jnp.concatenate(parts, axis=1)


def slot_start(listed, blocks, block, run, runs, reach):
    offset = lax.rem(lax.div(listed, blocks) - run + reach + runs, runs) - reach
    order = jnp.where(offset > 0, 2 * offset - 1, -2 * offset)
    return (order * blocks + lax.rem(listed, blocks)) * block


def pair_counts(list_ref, live_ref, src_ref, tgt_ref, block, run, runs, reach):
    blocks, slots, pairs = src_ref.shape
    candidates = (2 * reach + 1) * blocks
    point = lax.broadcasted_iota(jnp.int32, (block, pairs), 0)
    place = lax.broadcasted_iota(jnp.int32, (candidates * block, pairs), 0)
    rows = []
    for b in range(blocks):
        left = []
        right = []
        for s in range(slots):
            first = slot_start(list_ref[b, s], blocks, block, run, runs, reach)
            first = jnp.where(s < live_ref[0, b], first, -block)
            key = tgt_ref[b, s : s + 1, :] + first
            left.append(jnp.where(src_ref[b, s : s + 1, :] == point, 1.0, 0.0).astype(bf16))
            right.append(jnp.where(key == place, 1.0, 0.0).astype(bf16))
        rows.append(dot_nt(jnp.concatenate(left, axis=1), jnp.concatenate(right, axis=1)))
    return jnp.concatenate(rows, axis=0)


def moment_kernel(scale, xs_ref, xt_ref, w_ref, moment_ref):
    weight = w_ref[...]
    zs = project(xs_ref[...], weight)[0].astype(bf16)
    zt = project(xt_ref[...], weight)[0].astype(bf16)
    moment = (dot_tn(zs, zs) + dot_tn(zt, zt)) * scale
    at = 0
    for r in range(0, moment.shape[0], lane):
        for c in range(r, moment.shape[1], lane):
            moment_ref[at : at + lane, :] = moment[r : r + lane, c : c + lane].astype(bf16)
            at += lane


def own_kernel(
    runs, reach,
    run_ref, list_ref, live_ref, xs_ref, xt_ref, w_ref, src_ref, tgt_ref,
    unit_ref, inv_ref, count_ref, grad_ref, part_ref,
):
    weight = w_ref[...]
    src_unit, src_inv = project(xs_ref[...], weight)
    tgt_unit, tgt_inv = project(xt_ref[...], weight)
    zs = src_unit.astype(bf16)
    zt = tgt_unit.astype(bf16)
    unit_ref[...] = src_unit
    inv_ref[...] = jnp.broadcast_to(src_inv, inv_ref.shape)
    own = xs_ref.shape[0]
    block = own // src_ref.shape[0]
    counts = pair_counts(
        list_ref, live_ref, src_ref, tgt_ref, block, run_ref[0], runs, reach
    )
    count_ref[...] = counts[:, own:].astype(bf16)
    weights = pair_weights(zs, zt, counts[:, :own], block)
    grad_ref[...] = dot_nn(weights, zt)
    grad_zt = dot_tn(weights, zs) * inverse_sharpness
    part_ref[...] = dot_tn(xt_ref[...], back_norm(tgt_unit, tgt_inv, grad_zt))


def halo_kernel(
    nbrs, block, groups,
    grp_ref, xs_ref, w_ref, unit_ref, inv_ref, count_ref, grad_ref, part_ref, *refs,
):
    nbr_refs = refs[:nbrs]
    keep_ref, send_ref, total_ref = refs[nbrs:]
    weight = w_ref[...]
    rows = jnp.concatenate([r[...] for r in nbr_refs], axis=0)
    tgt_unit, tgt_inv = project(rows, weight)
    zt = tgt_unit.astype(bf16)
    src_unit = unit_ref[...]
    zs = src_unit.astype(bf16)
    weights = pair_weights(zs, zt, count_ref[...], block)
    grad_zs = (grad_ref[...] + dot_nn(weights, zt)) * inverse_sharpness
    grad_zt = dot_tn(weights, zs) * inverse_sharpness
    src_grad = back_norm(src_unit, inv_ref[:, :1], grad_zs)
    tgt_grad = back_norm(tgt_unit, tgt_inv, grad_zt)
    total_ref[...] = part_ref[...] + dot_tn(xs_ref[...], src_grad) + dot_tn(rows, tgt_grad)
    chunk = total_ref.shape[0] // groups
    me = grp_ref[0]
    keep_ref[...] = total_ref[pl.ds(pl.multiple_of(me * chunk, chunk), chunk), :]
    for k in range(1, groups):
        first = lax.rem(me + k, groups) * chunk
        send_ref[k - 1] = total_ref[pl.ds(pl.multiple_of(first, chunk), chunk), :].astype(bf16)


def unpack_ordered_kernel(packed_ref, out_ref):
    at = 0
    for r in range(0, out_ref.shape[0], lane):
        for c in range(r, out_ref.shape[1], lane):
            tile = packed_ref[at : at + lane, :].astype(f32)
            out_ref[r : r + lane, c : c + lane] = tile
            if c > r:
                out_ref[c : c + lane, r : r + lane] = tile.T
            at += lane


def unpack_kernel(run_ref, *refs):
    column_refs = refs[:-2]
    out_ref, packed_ref = refs[-2:]
    low = len(column_refs)
    rows = column_refs[0].shape[1]
    for m, ref in enumerate(column_refs):
        for k in range(ref.shape[0]):
            owner = lax.bitwise_xor(run_ref[0], k * low + m)
            packed_ref[pl.ds(pl.multiple_of(owner * rows, 16), rows), :] = ref[k]
    unpack_ordered_kernel(packed_ref, out_ref)


def sum_kernel(moved_ref, out_ref):
    total = moved_ref[0].astype(f32)
    for i in range(1, moved_ref.shape[0]):
        total = total + moved_ref[i].astype(f32)
    total = total.astype(bf16)
    for i in range(out_ref.shape[0]):
        out_ref[i] = total


def sum_pieces(moved, repeats):
    vmem = pl.BlockSpec(memory_space=pltpu.VMEM)
    return pl.pallas_call(
        sum_kernel,
        out_shape=jax.ShapeDtypeStruct((repeats,) + moved.shape[1:], moved.dtype),
        in_specs=[vmem],
        out_specs=vmem,
        compiler_params=room(8),
    )(moved)


def join_kernel(*refs):
    out_ref = refs[-1]
    for i, ref in enumerate(refs[:-1]):
        out_ref[i] = ref[0]


def join(pieces):
    vmem = pl.BlockSpec(memory_space=pltpu.VMEM)
    return pl.pallas_call(
        join_kernel,
        out_shape=jax.ShapeDtypeStruct((len(pieces),) + pieces[0].shape[1:], pieces[0].dtype),
        in_specs=[vmem] * len(pieces),
        out_specs=vmem,
        compiler_params=room(8),
    )(*pieces)


def body(src_feats, tgt_feats, proj_weight, match_blocks, match_count, pair_src, pair_tgt):
    xs = src_feats[0]
    xt = tgt_feats[0]
    points, width = xs.shape
    blocks = pair_src.shape[1]
    block = points // blocks
    runs = lax.axis_size("blk")
    groups = lax.axis_size("grp")
    reach = runs // 16
    run = lax.axis_index("blk")
    grp = lax.axis_index("grp")

    nbrs = []
    for k in range(1, reach + 1):
        nbrs.append(lax.ppermute(xt, "blk", [(i, (i - k) % runs) for i in range(runs)]))
        nbrs.append(lax.ppermute(xt, "blk", [(i, (i + k) % runs) for i in range(runs)]))

    tiles = width // lane
    packed_rows = tiles * (tiles + 1) // 2 * lane
    chunk = width // groups
    scale = width / (2.0 * points * runs)
    vmem = pl.BlockSpec(memory_space=pltpu.VMEM)
    smem = pl.BlockSpec(memory_space=pltpu.SMEM)

    packed = pl.pallas_call(
        functools.partial(moment_kernel, scale),
        out_shape=jax.ShapeDtypeStruct((packed_rows, lane), bf16),
        in_specs=[vmem] * 3,
        out_specs=vmem,
        compiler_params=room(16),
        name="moment",
    )(xs, xt, proj_weight)
    moved = lax.all_to_all(packed.reshape(runs, packed_rows // runs, lane), "blk", 0, 0)
    unit, inv, counts, grad, part = pl.pallas_call(
        functools.partial(own_kernel, runs, reach),
        out_shape=(
            jax.ShapeDtypeStruct((points, width), f32),
            jax.ShapeDtypeStruct((points, lane), f32),
            jax.ShapeDtypeStruct((points, 2 * reach * points), bf16),
            jax.ShapeDtypeStruct((points, width), f32),
            jax.ShapeDtypeStruct((width, width), f32),
        ),
        in_specs=[smem] * 3 + [vmem] * 5,
        out_specs=(vmem,) * 5,
        compiler_params=room(16 + 4 * reach),
        name="own",
    )(
        run.reshape(1), match_blocks[0], match_count, xs, xt, proj_weight,
        pair_src[0], pair_tgt[0],
    )
    keep, send = pl.pallas_call(
        functools.partial(halo_kernel, 2 * reach, block, groups),
        out_shape=(
            jax.ShapeDtypeStruct((chunk, width), f32),
            jax.ShapeDtypeStruct((groups - 1, chunk, width), bf16),
        ),
        in_specs=[smem] + [vmem] * (7 + 2 * reach),
        out_specs=(vmem, vmem),
        scratch_shapes=[pltpu.VMEM((width, width), f32)],
        compiler_params=room(16 + 8 * reach),
        name="halo",
    )(grp.reshape(1), xs, proj_weight, unit, inv, counts, grad, part, *nbrs)

    total = keep
    for k in range(1, groups):
        got = lax.ppermute(send[k - 1], "grp", [(i, (i + k) % groups) for i in range(groups)])
        total = total + got.astype(f32)
    spread = lax.all_to_all(total.astype(bf16).reshape(runs, chunk // runs, width), "blk", 0, 0)
    low = 1 << (runs.bit_length() // 2)
    mine = sum_pieces(moved, 1)
    pieces = [mine] + [
        lax.ppermute(mine, "blk", [(i, i ^ (k * low)) for i in range(runs)])
        for k in range(1, runs // low)
    ]
    column = join(pieces)
    mine = sum_pieces(spread, runs)
    whole = lax.all_to_all(mine, "blk", 0, 0)
    columns = [column] + [
        lax.ppermute(column, "blk", [(i, i ^ k) for i in range(runs)]) for k in range(1, low)
    ]
    rows = packed_rows // runs
    if rows % 16 == 0:
        covariance = pl.pallas_call(
            unpack_kernel,
            out_shape=jax.ShapeDtypeStruct((width, width), f32),
            in_specs=[smem] + [vmem] * low,
            out_specs=vmem,
            scratch_shapes=[pltpu.VMEM((packed_rows, lane), bf16)],
            compiler_params=room(12),
            name="unpack",
        )(run.reshape(1), *columns)
    else:
        owner = jnp.arange(runs, dtype=jnp.int32) ^ run
        found = jnp.stack(columns, axis=1).reshape(runs, rows, lane)
        ordered = jnp.take(found, owner, axis=0).reshape(packed_rows, lane)
        covariance = pl.pallas_call(
            unpack_ordered_kernel,
            out_shape=jax.ShapeDtypeStruct((width, width), f32),
            in_specs=[vmem],
            out_specs=vmem,
            compiler_params=room(12),
            name="unpack",
        )(ordered)
    half = whole.reshape(chunk, width)
    parts = [half]
    for k in range(1, groups):
        parts.append(lax.ppermute(half, "grp", [(i, (i - k) % groups) for i in range(groups)]))
    if groups == 2:
        low = jnp.where(grp == 0, parts[0], parts[1])
        high = jnp.where(grp == 0, parts[1], parts[0])
        weight_grad = jnp.concatenate([low, high], axis=0).astype(f32)
    else:
        stacked = jnp.stack(parts)
        place = (jnp.arange(groups, dtype=jnp.int32) - grp) % groups
        weight_grad = jnp.take(stacked, place, axis=0).reshape(width, width).astype(f32)
    return (weight_grad, covariance[None])


def solution(mesh):
    placed = (
        P("grp", "blk", None),
        P("grp", "blk", None),
        P(),
        P("grp", "blk", None),
        P("grp", "blk"),
        P("grp", "blk", None, None),
        P("grp", "blk", None, None),
    )
    return jax.shard_map(
        body, mesh=mesh, in_specs=placed, out_specs=(P(), P("grp", None, None)), check_vma=False
    )
```

```python
import functools
import jax
import jax.numpy as jnp
from jax import lax
from jax.experimental import pallas as pl
from jax.experimental.pallas import tpu as pltpu
from jax.sharding import PartitionSpec as P


inverse_sharpness = 2.5
logit_bound = 2.5
norm_eps = 1e-06
lane = 128


f32 = jnp.float32
bf16 = jnp.bfloat16


def dot_nn(a, b):
    return lax.dot_general(a, b, (((1,), (0,)), ((), ())), preferred_element_type=f32)


def dot_nt(a, b):
    return lax.dot_general(a, b, (((1,), (1,)), ((), ())), preferred_element_type=f32)


def dot_tn(a, b):
    return lax.dot_general(a, b, (((0,), (0,)), ((), ())), preferred_element_type=f32)


def room(mebibytes):
    return pltpu.CompilerParams(vmem_limit_bytes=mebibytes * 1024 * 1024)


def project(rows, weight):
    projected = dot_nn(rows, weight)
    inv_norm = lax.rsqrt(jnp.sum(projected * projected, axis=1, keepdims=True) + norm_eps)
    return projected * inv_norm, inv_norm


def back_norm(unit, inv_norm, grad):
    inner = jnp.sum(unit * grad, axis=1, keepdims=True)
    return ((grad - unit * inner) * inv_norm).astype(bf16)


def pair_weights(anchors, candidates, counts, block):
    logits = dot_nt(anchors, candidates)
    terms = jnp.exp(logits * inverse_sharpness - logit_bound)
    parts = []
    for first in range(0, candidates.shape[0], block):
        part = terms[:, first : first + block]
        count = counts[:, first : first + block].astype(f32)
        pairs = jnp.sum(count, axis=1, keepdims=True)
        total = jnp.sum(part, axis=1, keepdims=True)
        parts.append((part * (pairs / total) - count).astype(bf16))
    return jnp.concatenate(parts, axis=1)


def slot_start(listed, blocks, block, run, runs, reach):
    offset = lax.rem(lax.div(listed, blocks) - run + reach + runs, runs) - reach
    order = jnp.where(offset > 0, 2 * offset - 1, -2 * offset)
    return (order * blocks + lax.rem(listed, blocks)) * block


def pair_counts(list_ref, live_ref, src_ref, tgt_ref, block, run, runs, reach):
    blocks, slots, pairs = src_ref.shape
    candidates = (2 * reach + 1) * blocks
    point = lax.broadcasted_iota(jnp.int32, (block, pairs), 0)
    place = lax.broadcasted_iota(jnp.int32, (candidates * block, pairs), 0)
    rows = []
    for b in range(blocks):
        left = []
        right = []
        for s in range(slots):
            first = slot_start(list_ref[b, s], blocks, block, run, runs, reach)
            first = jnp.where(s < live_ref[0, b], first, -block)
            key = tgt_ref[b, s : s + 1, :] + first
            left.append(jnp.where(src_ref[b, s : s + 1, :] == point, 1.0, 0.0).astype(bf16))
            right.append(jnp.where(key == place, 1.0, 0.0).astype(bf16))
        rows.append(dot_nt(jnp.concatenate(left, axis=1), jnp.concatenate(right, axis=1)))
    return jnp.concatenate(rows, axis=0)


def load(pairs, sem):
    copies = [pltpu.make_async_copy(src, dst, sem.at[i]) for i, (src, dst) in enumerate(pairs)]
    for copy in copies:
        copy.start()
    return copies


def moment_kernel(far, near, scale, run_ref, xs_hbm, xt_hbm, w_hbm, *refs):
    out_refs = refs[:far]
    xs_ref, xt_ref, w_ref, packed_ref, sem = refs[far:]
    for copy in load(((w_hbm, w_ref), (xs_hbm, xs_ref), (xt_hbm, xt_ref)), sem):
        copy.wait()
    weight = w_ref[...]
    zs = project(xs_ref[...], weight)[0].astype(bf16)
    zt = project(xt_ref[...], weight)[0].astype(bf16)
    moment = (dot_tn(zs, zs) + dot_tn(zt, zt)) * scale
    at = 0
    for r in range(0, moment.shape[0], lane):
        for c in range(r, moment.shape[1], lane):
            packed_ref[at : at + lane, :] = moment[r : r + lane, c : c + lane].astype(bf16)
            at += lane
    if at < packed_ref.shape[0]:
        packed_ref[at:, :] = jnp.zeros((packed_ref.shape[0] - at, lane), bf16)
    rows = packed_ref.shape[0] // far
    place = lax.div(run_ref[0], near)
    for k in range(far):
        first = lax.bitwise_xor(place, k) * rows
        out_refs[k][...] = packed_ref[pl.ds(pl.multiple_of(first, 16), rows), :]


def own_kernel(
    runs, reach,
    run_ref, list_ref, live_ref, xs_ref, xt_ref, w_ref, src_ref, tgt_ref,
    unit_ref, inv_ref, count_ref, grad_ref, part_ref,
):
    weight = w_ref[...]
    src_unit, src_inv = project(xs_ref[...], weight)
    tgt_unit, tgt_inv = project(xt_ref[...], weight)
    zs = src_unit.astype(bf16)
    zt = tgt_unit.astype(bf16)
    unit_ref[...] = src_unit
    inv_ref[...] = jnp.broadcast_to(src_inv, inv_ref.shape)
    own = xs_ref.shape[0]
    block = own // src_ref.shape[0]
    counts = pair_counts(
        list_ref, live_ref, src_ref, tgt_ref, block, run_ref[0], runs, reach
    )
    count_ref[...] = counts[:, own:].astype(bf16)
    weights = pair_weights(zs, zt, counts[:, :own], block)
    grad_ref[...] = dot_nn(weights, zt)
    grad_zt = dot_tn(weights, zs) * inverse_sharpness
    part_ref[...] = dot_tn(xt_ref[...], back_norm(tgt_unit, tgt_inv, grad_zt))


def halo_kernel(
    reach, block, groups,
    grp_ref, xs_ref, w_ref, unit_ref, inv_ref, count_ref, grad_ref, part_ref, *refs,
):
    nbr_refs = refs[: 2 * reach]
    keep_ref, send_ref, total_ref = refs[2 * reach :]
    weight = w_ref[...]
    rows = jnp.concatenate([ref[...] for ref in nbr_refs], axis=0)
    tgt_unit, tgt_inv = project(rows, weight)
    zt = tgt_unit.astype(bf16)
    src_unit = unit_ref[...]
    zs = src_unit.astype(bf16)
    weights = pair_weights(zs, zt, count_ref[...], block)
    grad_zs = (grad_ref[...] + dot_nn(weights, zt)) * inverse_sharpness
    grad_zt = dot_tn(weights, zs) * inverse_sharpness
    src_grad = back_norm(src_unit, inv_ref[:, :1], grad_zs)
    tgt_grad = back_norm(tgt_unit, tgt_inv, grad_zt)
    total_ref[...] = part_ref[...] + dot_tn(xs_ref[...], src_grad) + dot_tn(rows, tgt_grad)
    chunk = total_ref.shape[0] // groups
    me = grp_ref[0]
    keep_ref[...] = total_ref[pl.ds(pl.multiple_of(me * chunk, chunk), chunk), :]
    for k in range(1, groups):
        first = lax.rem(me + k, groups) * chunk
        send_ref[k - 1] = total_ref[pl.ds(pl.multiple_of(first, chunk), chunk), :].astype(bf16)


def tree(parts):
    while len(parts) > 1:
        parts = [parts[i] + parts[i + 1] for i in range(0, len(parts), 2)]
    return parts[0]


def deal_kernel(near, groups, run_ref, *refs):
    keep_ref, *got_refs = refs[:groups]
    total_ref, sum_ref = refs[-2:]
    out_refs = refs[-2 - near : -2]
    piece_refs = refs[groups : -2 - near]
    total = keep_ref[...]
    for ref in got_refs:
        total = total + ref[...].astype(f32)
    total_ref[...] = total
    sum_ref[...] = tree([ref[...].astype(f32) for ref in piece_refs]).astype(bf16)
    place = lax.rem(run_ref[0], near)
    rows = total_ref.shape[0] // near
    below = sum_ref.shape[0] // near
    for k in range(near):
        owner = lax.bitwise_xor(place, k)
        part = total_ref[pl.ds(pl.multiple_of(owner * rows, rows), rows), :].astype(bf16)
        at = 0
        for c in range(0, total_ref.shape[1], lane):
            out_refs[k][at : at + rows, :] = part[:, c : c + lane]
            at += rows
        first = pl.multiple_of(owner * below, 16)
        out_refs[k][at : at + below, :] = sum_ref[pl.ds(first, below), :]


def near_kernel(*refs):
    refs[-1][...] = tree([ref[...].astype(f32) for ref in refs[:-1]]).astype(bf16)


def far_kernel(rows, *refs):
    out_ref = refs[-1]
    out_ref[:rows, :] = tree([ref[:rows, :].astype(f32) for ref in refs[:-1]]).astype(bf16)
    below = refs[0].shape[0] - rows
    for i, ref in enumerate(refs[:-1]):
        at = rows + i * below
        out_ref[at : at + below, :] = ref[rows:, :]


def gather_kernel(rows, *refs):
    out_ref = refs[-1]
    for i, ref in enumerate(refs[:-1]):
        out_ref[i * rows : (i + 1) * rows, :] = ref[:rows, :]


def unpack_kernel(near, far, skip, run_ref, *refs):
    column_refs = refs[:near]
    out_ref, packed_ref = refs[near:]
    rows = (column_refs[0].shape[0] - skip) // far
    for m, ref in enumerate(column_refs):
        for k in range(far):
            owner = lax.bitwise_xor(run_ref[0], k * near + m)
            at = skip + k * rows
            packed_ref[pl.ds(pl.multiple_of(owner * rows, 16), rows), :] = ref[at : at + rows, :]
    at = 0
    for r in range(0, out_ref.shape[0], lane):
        for c in range(r, out_ref.shape[1], lane):
            tile = packed_ref[at : at + lane, :].astype(f32)
            out_ref[r : r + lane, c : c + lane] = tile
            if c > r:
                out_ref[c : c + lane, r : r + lane] = tile.T
            at += lane


def place_kernel(near, run_ref, grp_ref, *refs):
    out_ref = refs[-1]
    groups = len(refs) - 1
    chunk = out_ref.shape[0] // groups
    rows = chunk // near
    place = lax.rem(run_ref[0], near)
    for j, ref in enumerate(refs[:-1]):
        base = lax.rem(grp_ref[0] + j, groups) * chunk
        at = 0
        for m in range(near):
            first = pl.multiple_of(base + lax.bitwise_xor(place, m) * rows, rows)
            for c in range(0, out_ref.shape[1], lane):
                out_ref[pl.ds(first, rows), c : c + lane] = ref[at : at + rows, :].astype(f32)
                at += rows


def swap(array, bits, runs):
    return lax.ppermute(array, "blk", [(i, i ^ bits) for i in range(runs)])


def small_call(kernel, shapes, specs, scratch=()):
    vmem = pl.BlockSpec(memory_space=pltpu.VMEM)
    many = isinstance(shapes, tuple)
    return pl.pallas_call(
        kernel,
        out_shape=shapes,
        in_specs=specs,
        out_specs=(vmem,) * len(shapes) if many else vmem,
        scratch_shapes=scratch,
        compiler_params=room(12),
    )


def body(src_feats, tgt_feats, proj_weight, match_blocks, match_count, pair_src, pair_tgt):
    xs = src_feats[0]
    xt = tgt_feats[0]
    points, width = xs.shape
    blocks = pair_src.shape[1]
    block = points // blocks
    runs = lax.axis_size("blk")
    groups = lax.axis_size("grp")
    reach = runs // 16
    run = lax.axis_index("blk")
    grp = lax.axis_index("grp")

    nbrs = []
    for k in range(1, reach + 1):
        nbrs.append(lax.ppermute(xt, "blk", [(i, (i - k) % runs) for i in range(runs)]))
        nbrs.append(lax.ppermute(xt, "blk", [(i, (i + k) % runs) for i in range(runs)]))

    tiles = width // lane
    near = 1 << (runs.bit_length() // 2)
    far = runs // near
    piece_rows = -(-tiles * (tiles + 1) // 2 * lane // (16 * runs)) * 16
    column_rows = near * piece_rows
    chunk = width // groups
    grad_rows = chunk // near * tiles
    scale = width / (2.0 * points * runs)
    vmem = pl.BlockSpec(memory_space=pltpu.VMEM)
    smem = pl.BlockSpec(memory_space=pltpu.SMEM)
    hbm = pl.BlockSpec(memory_space=pltpu.HBM)
    run_id = run.reshape(1)
    grp_id = grp.reshape(1)

    pieces = pl.pallas_call(
        functools.partial(moment_kernel, far, near, scale),
        out_shape=(jax.ShapeDtypeStruct((column_rows, lane), bf16),) * far,
        in_specs=[smem] + [hbm] * 3,
        out_specs=(vmem,) * far,
        scratch_shapes=[
            pltpu.VMEM((points, width), bf16),
            pltpu.VMEM((points, width), bf16),
            pltpu.VMEM((width, width), bf16),
            pltpu.VMEM((far * column_rows, lane), bf16),
            pltpu.SemaphoreType.DMA((3,)),
        ],
        compiler_params=room(16),
        name="moment",
    )(run_id, *(pltpu.with_memory_space_constraint(a, pltpu.HBM) for a in (xs, xt, proj_weight)))
    pieces = [pieces[0]] + [swap(pieces[k], k * near, runs) for k in range(1, far)]
    unit, inv, counts, grad, part = pl.pallas_call(
        functools.partial(own_kernel, runs, reach),
        out_shape=(
            jax.ShapeDtypeStruct((points, width), f32),
            jax.ShapeDtypeStruct((points, lane), f32),
            jax.ShapeDtypeStruct((points, 2 * reach * points), bf16),
            jax.ShapeDtypeStruct((points, width), f32),
            jax.ShapeDtypeStruct((width, width), f32),
        ),
        in_specs=[smem] * 3 + [vmem] * 5,
        out_specs=(vmem,) * 5,
        compiler_params=room(16 + 4 * reach),
        name="own",
    )(
        run_id, match_blocks[0], match_count, xs, xt, proj_weight,
        pair_src[0], pair_tgt[0],
    )
    keep, send = pl.pallas_call(
        functools.partial(halo_kernel, reach, block, groups),
        out_shape=(
            jax.ShapeDtypeStruct((chunk, width), f32),
            jax.ShapeDtypeStruct((groups - 1, chunk, width), bf16),
        ),
        in_specs=[smem] + [vmem] * (7 + 2 * reach),
        out_specs=(vmem, vmem),
        scratch_shapes=[pltpu.VMEM((width, width), f32)],
        compiler_params=room(16 + 8 * reach),
        name="halo",
    )(grp_id, xs, proj_weight, unit, inv, counts, grad, part, *nbrs)

    got = [
        lax.ppermute(send[k - 1], "grp", [(i, (i + k) % groups) for i in range(groups)])
        for k in range(1, groups)
    ]
    part_shape = jax.ShapeDtypeStruct((grad_rows + piece_rows, lane), bf16)
    parts = small_call(
        functools.partial(deal_kernel, near, groups),
        (part_shape,) * near,
        [smem] + [vmem] * (groups + far),
        [pltpu.VMEM((chunk, width), f32), pltpu.VMEM((column_rows, lane), bf16)],
    )(run_id, keep, *got, *pieces)
    parts = [parts[0]] + [swap(parts[k], k, runs) for k in range(1, near)]
    part = small_call(near_kernel, part_shape, [vmem] * near)(*parts)
    parts = [part] + [swap(part, k * near, runs) for k in range(1, far)]
    part = small_call(
        functools.partial(far_kernel, grad_rows),
        jax.ShapeDtypeStruct((grad_rows + far * piece_rows, lane), bf16),
        [vmem] * far,
    )(*parts)
    columns = [part] + [swap(part, k, runs) for k in range(1, near)]
    half = small_call(
        functools.partial(gather_kernel, grad_rows),
        jax.ShapeDtypeStruct((near * grad_rows, lane), bf16),
        [vmem] * near,
    )(*columns)
    halves = [half] + [
        lax.ppermute(half, "grp", [(i, (i - k) % groups) for i in range(groups)])
        for k in range(1, groups)
    ]
    covariance = small_call(
        functools.partial(unpack_kernel, near, far, grad_rows),
        jax.ShapeDtypeStruct((width, width), f32),
        [smem] + [vmem] * near,
        [pltpu.VMEM((far * column_rows, lane), bf16)],
    )(run_id, *columns)
    weight_grad = small_call(
        functools.partial(place_kernel, near),
        jax.ShapeDtypeStruct((width, width), f32),
        [smem] * 2 + [vmem] * groups,
    )(run_id, grp_id, *halves)
    return (weight_grad, covariance[None])


def solution(mesh):
    placed = (
        P("grp", "blk", None),
        P("grp", "blk", None),
        P(),
        P("grp", "blk", None),
        P("grp", "blk"),
        P("grp", "blk", None, None),
        P("grp", "blk", None, None),
    )
    return jax.shard_map(
        body, mesh=mesh, in_specs=placed, out_specs=(P(), P("grp", None, None)), check_vma=False
    )
```

```python
import functools
import jax
import jax.numpy as jnp
from jax import lax
from jax.experimental import pallas as pl
from jax.experimental.pallas import tpu as pltpu
from jax.sharding import PartitionSpec as P


inverse_sharpness = 2.5
logit_bound = 2.5
norm_eps = 1e-06
lane = 128


f32 = jnp.float32
bf16 = jnp.bfloat16


def dot_nn(a, b):
    return lax.dot_general(a, b, (((1,), (0,)), ((), ())), preferred_element_type=f32)


def dot_nt(a, b):
    return lax.dot_general(a, b, (((1,), (1,)), ((), ())), preferred_element_type=f32)


def dot_tn(a, b):
    return lax.dot_general(a, b, (((0,), (0,)), ((), ())), preferred_element_type=f32)


def room(mebibytes):
    return pltpu.CompilerParams(vmem_limit_bytes=mebibytes * 1024 * 1024)


def project(rows, weight):
    projected = dot_nn(rows, weight)
    inv_norm = lax.rsqrt(jnp.sum(projected * projected, axis=1, keepdims=True) + norm_eps)
    return projected * inv_norm, inv_norm


def back_norm(unit, inv_norm, grad):
    inner = jnp.sum(unit * grad, axis=1, keepdims=True)
    return ((grad - unit * inner) * inv_norm).astype(bf16)


def pair_weights(anchors, candidates, counts, block):
    logits = dot_nt(anchors, candidates)
    terms = jnp.exp(logits * inverse_sharpness - logit_bound)
    parts = []
    for first in range(0, candidates.shape[0], block):
        part = terms[:, first : first + block]
        count = counts[:, first : first + block].astype(f32)
        pairs = jnp.sum(count, axis=1, keepdims=True)
        total = jnp.sum(part, axis=1, keepdims=True)
        parts.append((part * (pairs / total) - count).astype(bf16))
    return jnp.concatenate(parts, axis=1)


def turn(k):
    return (k & -k).bit_length() - 1


def partners(k, odd, runs):
    pairs = [(i, (i + k) % runs) for i in range(runs) if (i >> turn(k)) % 2 == odd]
    return pairs + [(j, i) for i, j in pairs]


def slot_start(listed, blocks, block, run, runs, reach):
    offset = lax.rem(lax.div(listed, blocks) - run + reach + runs, runs) - reach
    order = 0
    for k in range(1, reach + 1):
        odd = lax.rem(lax.shift_right_logical(run, turn(k)), 2)
        order = jnp.where(offset == k, k + reach * odd, order)
        order = jnp.where(offset == -k, k + reach * (1 - odd), order)
    return (order * blocks + lax.rem(listed, blocks)) * block


def pair_counts(list_ref, live_ref, src_ref, tgt_ref, block, run, runs, reach):
    blocks, slots, pairs = src_ref.shape
    candidates = (2 * reach + 1) * blocks
    point = lax.broadcasted_iota(jnp.int32, (block, pairs), 0)
    place = lax.broadcasted_iota(jnp.int32, (candidates * block, pairs), 0)
    rows = []
    for b in range(blocks):
        left = []
        right = []
        for s in range(slots):
            first = slot_start(list_ref[b, s], blocks, block, run, runs, reach)
            first = jnp.where(s < live_ref[0, b], first, -block)
            key = tgt_ref[b, s : s + 1, :] + first
            left.append(jnp.where(src_ref[b, s : s + 1, :] == point, 1.0, 0.0).astype(bf16))
            right.append(jnp.where(key == place, 1.0, 0.0).astype(bf16))
        rows.append(dot_nt(jnp.concatenate(left, axis=1), jnp.concatenate(right, axis=1)))
    return jnp.concatenate(rows, axis=0)


def load(pairs, sem):
    copies = [pltpu.make_async_copy(src, dst, sem.at[i]) for i, (src, dst) in enumerate(pairs)]
    for copy in copies:
        copy.start()
    return copies


def moment_kernel(
    far, near, scale, run_ref, xs_hbm, xt_hbm, w_hbm, src_hbm, tgt_hbm, *refs
):
    out_refs = refs[:far]
    src_unit_ref, src_inv_ref, tgt_unit_ref, tgt_inv_ref, src_ref, tgt_ref = refs[far : far + 6]
    xs_ref, xt_ref, w_ref, packed_ref, sem = refs[far + 6 :]
    copies = load(
        (
            (w_hbm, w_ref),
            (xs_hbm, xs_ref),
            (xt_hbm, xt_ref),
            (src_hbm, src_ref),
            (tgt_hbm, tgt_ref),
        ),
        sem,
    )
    copies[0].wait()
    copies[1].wait()
    weight = w_ref[...]
    unit, inv_norm = project(xs_ref[...], weight)
    src_unit_ref[...] = unit
    src_inv_ref[...] = jnp.broadcast_to(inv_norm, src_inv_ref.shape)
    zs = unit.astype(bf16)
    copies[2].wait()
    unit, inv_norm = project(xt_ref[...], weight)
    tgt_unit_ref[...] = unit
    tgt_inv_ref[...] = jnp.broadcast_to(inv_norm, tgt_inv_ref.shape)
    zt = unit.astype(bf16)
    moment = (dot_tn(zs, zs) + dot_tn(zt, zt)) * scale
    at = 0
    for r in range(0, moment.shape[0], lane):
        for c in range(r, moment.shape[1], lane):
            packed_ref[at : at + lane, :] = moment[r : r + lane, c : c + lane].astype(bf16)
            at += lane
    if at < packed_ref.shape[0]:
        packed_ref[at:, :] = jnp.zeros((packed_ref.shape[0] - at, lane), bf16)
    rows = packed_ref.shape[0] // far
    place = lax.div(run_ref[0], near)
    for k in range(far):
        first = lax.bitwise_xor(place, k) * rows
        out_refs[k][...] = packed_ref[pl.ds(pl.multiple_of(first, 16), rows), :]
    copies[3].wait()
    copies[4].wait()


def own_kernel(
    runs, reach,
    run_ref, list_ref, live_ref, xt_ref, src_unit_ref, tgt_unit_ref, tgt_inv_ref, src_ref, tgt_ref,
    even_ref, odd_ref, grad_ref, part_ref,
):
    zs = src_unit_ref[...].astype(bf16)
    own = xt_ref.shape[0]
    block = own // src_ref.shape[0]
    counts = pair_counts(
        list_ref, live_ref, src_ref, tgt_ref, block, run_ref[0], runs, reach
    )
    far = own * (1 + reach)
    even_ref[...] = counts[:, own:far].astype(bf16)
    odd_ref[...] = counts[:, far:].astype(bf16)
    grad_ref[...], part_ref[...] = score(
        xt_ref[...], tgt_unit_ref[...], tgt_inv_ref[:, :1], zs, counts[:, :own], block
    )


def score(rows, unit, inv_norm, zs, counts, block):
    zt = unit.astype(bf16)
    weights = pair_weights(zs, zt, counts, block)
    grad_zt = dot_tn(weights, zs) * inverse_sharpness
    return dot_nn(weights, zt), dot_tn(rows, back_norm(unit, inv_norm, grad_zt))


def even_kernel(reach, block, w_ref, unit_ref, count_ref, grad_ref, part_ref, *refs):
    out_grad_ref, out_part_ref = refs[reach:]
    rows = jnp.concatenate([ref[...] for ref in refs[:reach]], axis=0)
    zs = unit_ref[...].astype(bf16)
    grad, part = score(rows, *project(rows, w_ref[...]), zs, count_ref[...], block)
    out_grad_ref[...] = grad_ref[...] + grad
    out_part_ref[...] = part_ref[...] + part


def odd_kernel(
    reach, block, groups,
    grp_ref, xs_ref, w_ref, unit_ref, inv_ref, count_ref, grad_ref, part_ref, *refs,
):
    keep_ref, send_ref, total_ref = refs[reach:]
    rows = jnp.concatenate([ref[...] for ref in refs[:reach]], axis=0)
    unit = unit_ref[...]
    zs = unit.astype(bf16)
    grad, part = score(rows, *project(rows, w_ref[...]), zs, count_ref[...], block)
    grad_zs = (grad_ref[...] + grad) * inverse_sharpness
    src_grad = back_norm(unit, inv_ref[:, :1], grad_zs)
    total_ref[...] = part_ref[...] + part + dot_tn(xs_ref[...], src_grad)
    chunk = total_ref.shape[0] // groups
    me = grp_ref[0]
    keep_ref[...] = total_ref[pl.ds(pl.multiple_of(me * chunk, chunk), chunk), :]
    for k in range(1, groups):
        first = lax.rem(me + k, groups) * chunk
        send_ref[k - 1] = total_ref[pl.ds(pl.multiple_of(first, chunk), chunk), :].astype(bf16)


def tree(parts):
    while len(parts) > 1:
        parts = [parts[i] + parts[i + 1] for i in range(0, len(parts), 2)]
    return parts[0]


def deal_kernel(near, groups, run_ref, *refs):
    keep_ref, *got_refs = refs[:groups]
    total_ref, sum_ref = refs[-2:]
    out_refs = refs[-2 - near : -2]
    piece_refs = refs[groups : -2 - near]
    total = keep_ref[...]
    for ref in got_refs:
        total = total + ref[...].astype(f32)
    total_ref[...] = total
    sum_ref[...] = tree([ref[...].astype(f32) for ref in piece_refs]).astype(bf16)
    place = lax.rem(run_ref[0], near)
    rows = total_ref.shape[0] // near
    below = sum_ref.shape[0] // near
    for k in range(near):
        owner = lax.bitwise_xor(place, k)
        part = total_ref[pl.ds(pl.multiple_of(owner * rows, rows), rows), :].astype(bf16)
        at = 0
        for c in range(0, total_ref.shape[1], lane):
            out_refs[k][at : at + rows, :] = part[:, c : c + lane]
            at += rows
        first = pl.multiple_of(owner * below, 16)
        out_refs[k][at : at + below, :] = sum_ref[pl.ds(first, below), :]


def near_kernel(*refs):
    refs[-1][...] = tree([ref[...].astype(f32) for ref in refs[:-1]]).astype(bf16)


def far_kernel(rows, *refs):
    out_ref = refs[-1]
    out_ref[:rows, :] = tree([ref[:rows, :].astype(f32) for ref in refs[:-1]]).astype(bf16)
    below = refs[0].shape[0] - rows
    for i, ref in enumerate(refs[:-1]):
        at = rows + i * below
        out_ref[at : at + below, :] = ref[rows:, :]


def gather_kernel(rows, *refs):
    out_ref = refs[-1]
    for i, ref in enumerate(refs[:-1]):
        out_ref[i * rows : (i + 1) * rows, :] = ref[:rows, :]


def unpack_kernel(near, far, skip, run_ref, *refs):
    column_refs = refs[:near]
    out_ref, packed_ref = refs[near:]
    rows = (column_refs[0].shape[0] - skip) // far
    for m, ref in enumerate(column_refs):
        for k in range(far):
            owner = lax.bitwise_xor(run_ref[0], k * near + m)
            at = skip + k * rows
            packed_ref[pl.ds(pl.multiple_of(owner * rows, 16), rows), :] = ref[at : at + rows, :]
    at = 0
    for r in range(0, out_ref.shape[0], lane):
        for c in range(r, out_ref.shape[1], lane):
            tile = packed_ref[at : at + lane, :].astype(f32)
            out_ref[r : r + lane, c : c + lane] = tile
            if c > r:
                out_ref[c : c + lane, r : r + lane] = tile.T
            at += lane


def place_kernel(near, run_ref, grp_ref, *refs):
    out_ref = refs[-1]
    groups = len(refs) - 1
    chunk = out_ref.shape[0] // groups
    rows = chunk // near
    place = lax.rem(run_ref[0], near)
    for j, ref in enumerate(refs[:-1]):
        base = lax.rem(grp_ref[0] + j, groups) * chunk
        at = 0
        for m in range(near):
            first = pl.multiple_of(base + lax.bitwise_xor(place, m) * rows, rows)
            for c in range(0, out_ref.shape[1], lane):
                out_ref[pl.ds(first, rows), c : c + lane] = ref[at : at + rows, :].astype(f32)
                at += rows


def swap(array, bits, runs):
    return lax.ppermute(array, "blk", [(i, i ^ bits) for i in range(runs)])


def small_call(kernel, shapes, specs, scratch=()):
    vmem = pl.BlockSpec(memory_space=pltpu.VMEM)
    many = isinstance(shapes, tuple)
    return pl.pallas_call(
        kernel,
        out_shape=shapes,
        in_specs=specs,
        out_specs=(vmem,) * len(shapes) if many else vmem,
        scratch_shapes=scratch,
        compiler_params=room(12),
    )


def body(src_feats, tgt_feats, proj_weight, match_blocks, match_count, pair_src, pair_tgt):
    xs = src_feats[0]
    xt = tgt_feats[0]
    points, width = xs.shape
    blocks = pair_src.shape[1]
    block = points // blocks
    runs = lax.axis_size("blk")
    groups = lax.axis_size("grp")
    reach = runs // 16
    run = lax.axis_index("blk")
    grp = lax.axis_index("grp")

    hops = range(1, reach + 1)
    odd = [lax.ppermute(xt, "blk", partners(k, 1, runs)) for k in hops]
    even = [lax.ppermute(xt, "blk", partners(k, 0, runs)) for k in hops]

    tiles = width // lane
    near = 1 << (runs.bit_length() // 2)
    far = runs // near
    piece_rows = -(-tiles * (tiles + 1) // 2 * lane // (16 * runs)) * 16
    column_rows = near * piece_rows
    chunk = width // groups
    grad_rows = chunk // near * tiles
    scale = width / (2.0 * points * runs)
    vmem = pl.BlockSpec(memory_space=pltpu.VMEM)
    smem = pl.BlockSpec(memory_space=pltpu.SMEM)
    hbm = pl.BlockSpec(memory_space=pltpu.HBM)
    run_id = run.reshape(1)
    grp_id = grp.reshape(1)

    far_away = [
        pltpu.with_memory_space_constraint(array, pltpu.HBM)
        for array in (xs, xt, proj_weight, pair_src[0], pair_tgt[0])
    ]
    *pieces, unit, inv, tgt_unit, tgt_inv, sources, targets = pl.pallas_call(
        functools.partial(moment_kernel, far, near, scale),
        out_shape=(jax.ShapeDtypeStruct((column_rows, lane), bf16),) * far
        + (jax.ShapeDtypeStruct((points, width), f32), jax.ShapeDtypeStruct((points, lane), f32))
        * 2
        + (jax.ShapeDtypeStruct(pair_src.shape[1:], jnp.int32),) * 2,
        in_specs=[smem] + [hbm] * 5,
        out_specs=(vmem,) * (far + 6),
        scratch_shapes=[
            pltpu.VMEM((points, width), bf16),
            pltpu.VMEM((points, width), bf16),
            pltpu.VMEM((width, width), bf16),
            pltpu.VMEM((far * column_rows, lane), bf16),
            pltpu.SemaphoreType.DMA((5,)),
        ],
        compiler_params=room(16),
        name="moment",
    )(run_id, *far_away)
    pieces = [pieces[0]] + [swap(pieces[k], k * near, runs) for k in range(1, far)]
    even_count, odd_count, grad, part = pl.pallas_call(
        functools.partial(own_kernel, runs, reach),
        out_shape=(
            jax.ShapeDtypeStruct((points, reach * points), bf16),
            jax.ShapeDtypeStruct((points, reach * points), bf16),
            jax.ShapeDtypeStruct((points, width), f32),
            jax.ShapeDtypeStruct((width, width), f32),
        ),
        in_specs=[smem] * 3 + [vmem] * 6,
        out_specs=(vmem,) * 4,
        compiler_params=room(16 + 4 * reach),
        name="own",
    )(
        run_id, match_blocks[0], match_count, xt, unit, tgt_unit, tgt_inv, sources, targets
    )
    grad, part = pl.pallas_call(
        functools.partial(even_kernel, reach, block),
        out_shape=(
            jax.ShapeDtypeStruct((points, width), f32),
            jax.ShapeDtypeStruct((width, width), f32),
        ),
        in_specs=[vmem] * (5 + reach),
        out_specs=(vmem, vmem),
        compiler_params=room(16 + 4 * reach),
        name="even",
    )(proj_weight, unit, even_count, grad, part, *even)
    keep, send = pl.pallas_call(
        functools.partial(odd_kernel, reach, block, groups),
        out_shape=(
            jax.ShapeDtypeStruct((chunk, width), f32),
            jax.ShapeDtypeStruct((groups - 1, chunk, width), bf16),
        ),
        in_specs=[smem] + [vmem] * (7 + reach),
        out_specs=(vmem, vmem),
        scratch_shapes=[pltpu.VMEM((width, width), f32)],
        compiler_params=room(16 + 4 * reach),
        name="odd",
    )(grp_id, xs, proj_weight, unit, inv, odd_count, grad, part, *odd)

    got = [
        lax.ppermute(send[k - 1], "grp", [(i, (i + k) % groups) for i in range(groups)])
        for k in range(1, groups)
    ]
    part_shape = jax.ShapeDtypeStruct((grad_rows + piece_rows, lane), bf16)
    parts = small_call(
        functools.partial(deal_kernel, near, groups),
        (part_shape,) * near,
        [smem] + [vmem] * (groups + far),
        [pltpu.VMEM((chunk, width), f32), pltpu.VMEM((column_rows, lane), bf16)],
    )(run_id, keep, *got, *pieces)
    parts = [parts[0]] + [swap(parts[k], k, runs) for k in range(1, near)]
    part = small_call(near_kernel, part_shape, [vmem] * near)(*parts)
    parts = [part] + [swap(part, k * near, runs) for k in range(1, far)]
    part = small_call(
        functools.partial(far_kernel, grad_rows),
        jax.ShapeDtypeStruct((grad_rows + far * piece_rows, lane), bf16),
        [vmem] * far,
    )(*parts)
    columns = [part] + [swap(part, k, runs) for k in range(1, near)]
    half = small_call(
        functools.partial(gather_kernel, grad_rows),
        jax.ShapeDtypeStruct((near * grad_rows, lane), bf16),
        [vmem] * near,
    )(*columns)
    halves = [half] + [
        lax.ppermute(half, "grp", [(i, (i - k) % groups) for i in range(groups)])
        for k in range(1, groups)
    ]
    covariance = small_call(
        functools.partial(unpack_kernel, near, far, grad_rows),
        jax.ShapeDtypeStruct((width, width), f32),
        [smem] + [vmem] * near,
        [pltpu.VMEM((far * column_rows, lane), bf16)],
    )(run_id, *columns)
    weight_grad = small_call(
        functools.partial(place_kernel, near),
        jax.ShapeDtypeStruct((width, width), f32),
        [smem] * 2 + [vmem] * groups,
    )(run_id, grp_id, *halves)
    return (weight_grad, covariance[None])


def solution(mesh):
    placed = (
        P("grp", "blk", None),
        P("grp", "blk", None),
        P(),
        P("grp", "blk", None),
        P("grp", "blk"),
        P("grp", "blk", None, None),
        P("grp", "blk", None, None),
    )
    return jax.shard_map(
        body, mesh=mesh, in_specs=placed, out_specs=(P(), P("grp", None, None)), check_vma=False
    )
```

```python
import functools
import jax
import jax.numpy as jnp
from jax import lax
from jax.experimental import pallas as pl
from jax.experimental.pallas import tpu as pltpu
from jax.sharding import PartitionSpec as P


inverse_sharpness = 2.5
logit_bound = 2.5
norm_eps = 1e-06
lane = 128


f32 = jnp.float32
bf16 = jnp.bfloat16


def dot_nn(a, b):
    return lax.dot_general(a, b, (((1,), (0,)), ((), ())), preferred_element_type=f32)


def dot_nt(a, b):
    return lax.dot_general(a, b, (((1,), (1,)), ((), ())), preferred_element_type=f32)


def dot_tn(a, b):
    return lax.dot_general(a, b, (((0,), (0,)), ((), ())), preferred_element_type=f32)


def room(mebibytes):
    return pltpu.CompilerParams(vmem_limit_bytes=mebibytes * 1024 * 1024)


def project(rows, weight):
    projected = dot_nn(rows, weight)
    inv_norm = lax.rsqrt(jnp.sum(projected * projected, axis=1, keepdims=True) + norm_eps)
    return projected * inv_norm, inv_norm


def back_norm(unit, inv_norm, grad):
    inner = jnp.sum(unit * grad, axis=1, keepdims=True)
    return ((grad - unit * inner) * inv_norm).astype(bf16)


def pair_weights(anchors, candidates, counts, block):
    logits = dot_nt(anchors, candidates)
    terms = jnp.exp(logits * inverse_sharpness - logit_bound)
    parts = []
    for first in range(0, candidates.shape[0], block):
        part = terms[:, first : first + block]
        count = counts[:, first : first + block].astype(f32)
        pairs = jnp.sum(count, axis=1, keepdims=True)
        total = jnp.sum(part, axis=1, keepdims=True)
        parts.append((part * (pairs / total) - count).astype(bf16))
    return jnp.concatenate(parts, axis=1)


def split(runs):
    near = 1 << (runs.bit_length() // 2)
    return near, runs // near


def turn(k):
    return (k & -k).bit_length() - 1


def partners(k, odd, runs):
    pairs = [(i, (i + k) % runs) for i in range(runs) if (i >> turn(k)) % 2 == odd]
    return pairs + [(j, i) for i, j in pairs]


def slot_start(listed, blocks, block, run, runs, reach):
    offset = lax.rem(lax.div(listed, blocks) - run + reach + runs, runs) - reach
    order = 0
    for k in range(1, reach + 1):
        odd = lax.rem(lax.shift_right_logical(run, turn(k)), 2)
        order = jnp.where(offset == k, k + reach * odd, order)
        order = jnp.where(offset == -k, k + reach * (1 - odd), order)
    return (order * blocks + lax.rem(listed, blocks)) * block


def pair_counts(list_ref, live_ref, src_ref, tgt_ref, block, run, runs, reach):
    blocks, slots, pairs = src_ref.shape
    candidates = (2 * reach + 1) * blocks
    point = lax.broadcasted_iota(jnp.int32, (block, pairs), 0)
    place = lax.broadcasted_iota(jnp.int32, (candidates * block, pairs), 0)
    rows = []
    for b in range(blocks):
        left = []
        right = []
        for s in range(slots):
            first = slot_start(list_ref[b, s], blocks, block, run, runs, reach)
            first = jnp.where(s < live_ref[0, b], first, -block)
            key = tgt_ref[b, s : s + 1, :] + first
            left.append(jnp.where(src_ref[b, s : s + 1, :] == point, 1.0, 0.0).astype(bf16))
            right.append(jnp.where(key == place, 1.0, 0.0).astype(bf16))
        rows.append(dot_nt(jnp.concatenate(left, axis=1), jnp.concatenate(right, axis=1)))
    return jnp.concatenate(rows, axis=0)


def load(pairs, sem):
    copies = [pltpu.make_async_copy(src, dst, sem.at[i]) for i, (src, dst) in enumerate(pairs)]
    for copy in copies:
        copy.start()
    return copies


def moment_kernel(
    far, near, scale, run_ref, xs_hbm, xt_hbm, w_hbm, src_hbm, tgt_hbm, *refs
):
    out_refs = refs[:far]
    src_unit_ref, src_inv_ref, tgt_unit_ref, tgt_inv_ref, src_ref, tgt_ref = refs[far : far + 6]
    xs_ref, xt_ref, w_ref, packed_ref, sem = refs[far + 6 :]
    copies = load(
        (
            (w_hbm, w_ref),
            (xs_hbm, xs_ref),
            (xt_hbm, xt_ref),
            (src_hbm, src_ref),
            (tgt_hbm, tgt_ref),
        ),
        sem,
    )
    copies[0].wait()
    copies[1].wait()
    weight = w_ref[...]
    unit, inv_norm = project(xs_ref[...], weight)
    src_unit_ref[...] = unit
    src_inv_ref[...] = jnp.broadcast_to(inv_norm, src_inv_ref.shape)
    zs = unit.astype(bf16)
    copies[2].wait()
    unit, inv_norm = project(xt_ref[...], weight)
    tgt_unit_ref[...] = unit
    tgt_inv_ref[...] = jnp.broadcast_to(inv_norm, tgt_inv_ref.shape)
    zt = unit.astype(bf16)
    moment = (dot_tn(zs, zs) + dot_tn(zt, zt)) * scale
    at = 0
    for r in range(0, moment.shape[0], lane):
        for c in range(r, moment.shape[1], lane):
            packed_ref[at : at + lane, :] = moment[r : r + lane, c : c + lane].astype(bf16)
            at += lane
    if at < packed_ref.shape[0]:
        packed_ref[at:, :] = jnp.zeros((packed_ref.shape[0] - at, lane), bf16)
    rows = packed_ref.shape[0] // far
    place = lax.div(run_ref[0], near)
    for k in range(far):
        first = lax.bitwise_xor(place, k) * rows
        out_refs[k][...] = packed_ref[pl.ds(pl.multiple_of(first, 16), rows), :]
    copies[3].wait()
    copies[4].wait()


def own_kernel(
    runs, reach,
    run_ref, list_ref, live_ref, xt_ref, src_unit_ref, tgt_unit_ref, tgt_inv_ref, src_ref, tgt_ref,
    count_ref, grad_ref, part_ref,
):
    zs = src_unit_ref[...].astype(bf16)
    own = xt_ref.shape[0]
    block = own // src_ref.shape[0]
    counts = pair_counts(
        list_ref, live_ref, src_ref, tgt_ref, block, run_ref[0], runs, reach
    )
    count_ref[...] = counts[:, own:].astype(bf16)
    grad_ref[...], part_ref[...] = score(
        xt_ref[...], tgt_unit_ref[...], tgt_inv_ref[:, :1], zs, counts[:, :own], block
    )


def score(rows, unit, inv_norm, zs, counts, block):
    zt = unit.astype(bf16)
    weights = pair_weights(zs, zt, counts, block)
    grad_zt = dot_tn(weights, zs) * inverse_sharpness
    return dot_nn(weights, zt), dot_tn(rows, back_norm(unit, inv_norm, grad_zt))


def halo_kernel(
    nbrs, block, groups,
    grp_ref, xs_ref, w_ref, unit_ref, inv_ref, count_ref, grad_ref, part_ref, *refs,
):
    keep_ref, send_ref, total_ref = refs[nbrs:]
    rows = jnp.concatenate([ref[...] for ref in refs[:nbrs]], axis=0)
    unit = unit_ref[...]
    zs = unit.astype(bf16)
    grad, part = score(rows, *project(rows, w_ref[...]), zs, count_ref[...], block)
    grad_zs = (grad_ref[...] + grad) * inverse_sharpness
    src_grad = back_norm(unit, inv_ref[:, :1], grad_zs)
    total_ref[...] = part_ref[...] + part + dot_tn(xs_ref[...], src_grad)
    chunk = total_ref.shape[0] // groups
    me = grp_ref[0]
    keep_ref[...] = total_ref[pl.ds(pl.multiple_of(me * chunk, chunk), chunk), :]
    for k in range(1, groups):
        first = lax.rem(me + k, groups) * chunk
        send_ref[k - 1] = total_ref[pl.ds(pl.multiple_of(first, chunk), chunk), :].astype(bf16)


def tree(parts):
    while len(parts) > 1:
        parts = [parts[i] + parts[i + 1] for i in range(0, len(parts), 2)]
    return parts[0]


def deal_kernel(near, groups, run_ref, *refs):
    keep_ref, *got_refs = refs[:groups]
    total_ref, sum_ref = refs[-2:]
    out_refs = refs[-2 - near : -2]
    piece_refs = refs[groups : -2 - near]
    total = keep_ref[...]
    for ref in got_refs:
        total = total + ref[...].astype(f32)
    total_ref[...] = total
    sum_ref[...] = tree([ref[...].astype(f32) for ref in piece_refs]).astype(bf16)
    place = lax.rem(run_ref[0], near)
    rows = total_ref.shape[0] // near
    below = sum_ref.shape[0] // near
    for k in range(near):
        owner = lax.bitwise_xor(place, k)
        part = total_ref[pl.ds(pl.multiple_of(owner * rows, rows), rows), :].astype(bf16)
        at = 0
        for c in range(0, total_ref.shape[1], lane):
            out_refs[k][at : at + rows, :] = part[:, c : c + lane]
            at += rows
        first = pl.multiple_of(owner * below, 16)
        out_refs[k][at : at + below, :] = sum_ref[pl.ds(first, below), :]


def near_kernel(*refs):
    refs[-1][...] = tree([ref[...].astype(f32) for ref in refs[:-1]]).astype(bf16)


def far_kernel(rows, *refs):
    out_ref = refs[-1]
    out_ref[:rows, :] = tree([ref[:rows, :].astype(f32) for ref in refs[:-1]]).astype(bf16)
    below = refs[0].shape[0] - rows
    for i, ref in enumerate(refs[:-1]):
        at = rows + i * below
        out_ref[at : at + below, :] = ref[rows:, :]


def gather_kernel(rows, *refs):
    out_ref = refs[-1]
    for i, ref in enumerate(refs[:-1]):
        out_ref[i * rows : (i + 1) * rows, :] = ref[:rows, :]


def unpack_kernel(near, far, skip, run_ref, *refs):
    column_refs = refs[:near]
    out_ref, packed_ref = refs[near:]
    rows = (column_refs[0].shape[0] - skip) // far
    for m, ref in enumerate(column_refs):
        for k in range(far):
            owner = lax.bitwise_xor(run_ref[0], k * near + m)
            at = skip + k * rows
            packed_ref[pl.ds(pl.multiple_of(owner * rows, 16), rows), :] = ref[at : at + rows, :]
    at = 0
    for r in range(0, out_ref.shape[0], lane):
        for c in range(r, out_ref.shape[1], lane):
            tile = packed_ref[at : at + lane, :].astype(f32)
            out_ref[r : r + lane, c : c + lane] = tile
            if c > r:
                out_ref[c : c + lane, r : r + lane] = tile.T
            at += lane


def place_kernel(near, run_ref, grp_ref, *refs):
    out_ref = refs[-1]
    groups = len(refs) - 1
    chunk = out_ref.shape[0] // groups
    rows = chunk // near
    place = lax.rem(run_ref[0], near)
    for j, ref in enumerate(refs[:-1]):
        base = lax.rem(grp_ref[0] + j, groups) * chunk
        at = 0
        for m in range(near):
            first = pl.multiple_of(base + lax.bitwise_xor(place, m) * rows, rows)
            for c in range(0, out_ref.shape[1], lane):
                out_ref[pl.ds(first, rows), c : c + lane] = ref[at : at + rows, :].astype(f32)
                at += rows


def swap(array, bits, runs):
    return lax.ppermute(array, "blk", [(i, i ^ bits) for i in range(runs)])


def small_call(kernel, shapes, specs, scratch=()):
    vmem = pl.BlockSpec(memory_space=pltpu.VMEM)
    many = isinstance(shapes, tuple)
    return pl.pallas_call(
        kernel,
        out_shape=shapes,
        in_specs=specs,
        out_specs=(vmem,) * len(shapes) if many else vmem,
        scratch_shapes=scratch,
        compiler_params=room(12),
    )


def body(src_feats, tgt_feats, proj_weight, match_blocks, match_count, pair_src, pair_tgt):
    xs = src_feats[0]
    xt = tgt_feats[0]
    points, width = xs.shape
    blocks = pair_src.shape[1]
    block = points // blocks
    runs = lax.axis_size("blk")
    groups = lax.axis_size("grp")
    reach = runs // 16
    run = lax.axis_index("blk")
    grp = lax.axis_index("grp")

    hops = range(1, reach + 1)
    odd = [lax.ppermute(xt, "blk", partners(k, 1, runs)) for k in hops]
    even = [lax.ppermute(xt, "blk", partners(k, 0, runs)) for k in hops]

    tiles = width // lane
    near, far = split(runs)
    piece_rows = -(-tiles * (tiles + 1) // 2 * lane // (16 * runs)) * 16
    column_rows = near * piece_rows
    chunk = width // groups
    grad_rows = chunk // near * tiles
    scale = width / (2.0 * points * runs)
    vmem = pl.BlockSpec(memory_space=pltpu.VMEM)
    smem = pl.BlockSpec(memory_space=pltpu.SMEM)
    hbm = pl.BlockSpec(memory_space=pltpu.HBM)
    run_id = run.reshape(1)
    grp_id = grp.reshape(1)

    far_away = [
        pltpu.with_memory_space_constraint(array, pltpu.HBM)
        for array in (xs, xt, proj_weight, pair_src[0], pair_tgt[0])
    ]
    *pieces, unit, inv, tgt_unit, tgt_inv, sources, targets = pl.pallas_call(
        functools.partial(moment_kernel, far, near, scale),
        out_shape=(jax.ShapeDtypeStruct((column_rows, lane), bf16),) * far
        + (jax.ShapeDtypeStruct((points, width), f32), jax.ShapeDtypeStruct((points, lane), f32))
        * 2
        + (jax.ShapeDtypeStruct(pair_src.shape[1:], jnp.int32),) * 2,
        in_specs=[smem] + [hbm] * 5,
        out_specs=(vmem,) * (far + 6),
        scratch_shapes=[
            pltpu.VMEM((points, width), bf16),
            pltpu.VMEM((points, width), bf16),
            pltpu.VMEM((width, width), bf16),
            pltpu.VMEM((far * column_rows, lane), bf16),
            pltpu.SemaphoreType.DMA((5,)),
        ],
        compiler_params=room(16),
        name="moment",
    )(run_id, *far_away)
    pieces = [pieces[0]] + [swap(pieces[k], k * near, runs) for k in range(1, far)]
    counts, grad, part = pl.pallas_call(
        functools.partial(own_kernel, runs, reach),
        out_shape=(
            jax.ShapeDtypeStruct((points, 2 * reach * points), bf16),
            jax.ShapeDtypeStruct((points, width), f32),
            jax.ShapeDtypeStruct((width, width), f32),
        ),
        in_specs=[smem] * 3 + [vmem] * 6,
        out_specs=(vmem,) * 3,
        compiler_params=room(16 + 4 * reach),
        name="own",
    )(
        run_id, match_blocks[0], match_count, xt, unit, tgt_unit, tgt_inv, sources, targets
    )
    keep, send = pl.pallas_call(
        functools.partial(halo_kernel, 2 * reach, block, groups),
        out_shape=(
            jax.ShapeDtypeStruct((chunk, width), f32),
            jax.ShapeDtypeStruct((groups - 1, chunk, width), bf16),
        ),
        in_specs=[smem] + [vmem] * (7 + 2 * reach),
        out_specs=(vmem, vmem),
        scratch_shapes=[pltpu.VMEM((width, width), f32)],
        compiler_params=room(16 + 4 * reach),
        name="halo",
    )(grp_id, xs, proj_weight, unit, inv, counts, grad, part, *even, *odd)

    got = [
        lax.ppermute(send[k - 1], "grp", [(i, (i + k) % groups) for i in range(groups)])
        for k in range(1, groups)
    ]
    part_shape = jax.ShapeDtypeStruct((grad_rows + piece_rows, lane), bf16)
    parts = small_call(
        functools.partial(deal_kernel, near, groups),
        (part_shape,) * near,
        [smem] + [vmem] * (groups + far),
        [pltpu.VMEM((chunk, width), f32), pltpu.VMEM((column_rows, lane), bf16)],
    )(run_id, keep, *got, *pieces)
    parts = [parts[0]] + [swap(parts[k], k, runs) for k in range(1, near)]
    part = small_call(near_kernel, part_shape, [vmem] * near)(*parts)
    parts = [part] + [swap(part, k * near, runs) for k in range(1, far)]
    part = small_call(
        functools.partial(far_kernel, grad_rows),
        jax.ShapeDtypeStruct((grad_rows + far * piece_rows, lane), bf16),
        [vmem] * far,
    )(*parts)
    columns = [part] + [swap(part, k, runs) for k in range(1, near)]
    half = small_call(
        functools.partial(gather_kernel, grad_rows),
        jax.ShapeDtypeStruct((near * grad_rows, lane), bf16),
        [vmem] * near,
    )(*columns)
    halves = [half] + [
        lax.ppermute(half, "grp", [(i, (i - k) % groups) for i in range(groups)])
        for k in range(1, groups)
    ]
    covariance = small_call(
        functools.partial(unpack_kernel, near, far, grad_rows),
        jax.ShapeDtypeStruct((width, width), f32),
        [smem] + [vmem] * near,
        [pltpu.VMEM((far * column_rows, lane), bf16)],
    )(run_id, *columns)
    weight_grad = small_call(
        functools.partial(place_kernel, near),
        jax.ShapeDtypeStruct((width, width), f32),
        [smem] * 2 + [vmem] * groups,
    )(run_id, grp_id, *halves)
    return (weight_grad, covariance[None])


def solution(mesh):
    placed = (
        P("grp", "blk", None),
        P("grp", "blk", None),
        P(),
        P("grp", "blk", None),
        P("grp", "blk"),
        P("grp", "blk", None, None),
        P("grp", "blk", None, None),
    )
    return jax.shard_map(
        body, mesh=mesh, in_specs=placed, out_specs=(P(), P("grp", None, None)), check_vma=False
    )
```

```python
import functools
import jax
import jax.numpy as jnp
from jax import lax
from jax.experimental import pallas as pl
from jax.experimental.pallas import tpu as pltpu
from jax.sharding import PartitionSpec as P


inverse_sharpness = 2.5
logit_bound = 2.5
norm_eps = 1e-06
lane = 128


f32 = jnp.float32
bf16 = jnp.bfloat16


def dot_nn(a, b):
    return lax.dot_general(a, b, (((1,), (0,)), ((), ())), preferred_element_type=f32)


def dot_nt(a, b):
    return lax.dot_general(a, b, (((1,), (1,)), ((), ())), preferred_element_type=f32)


def dot_tn(a, b):
    return lax.dot_general(a, b, (((0,), (0,)), ((), ())), preferred_element_type=f32)


def room(mebibytes):
    return pltpu.CompilerParams(vmem_limit_bytes=mebibytes * 1024 * 1024)


def project(rows, weight):
    projected = dot_nn(rows, weight)
    inv_norm = lax.rsqrt(jnp.sum(projected * projected, axis=1, keepdims=True) + norm_eps)
    return projected * inv_norm, inv_norm


def back_norm(unit, inv_norm, grad):
    inner = jnp.sum(unit * grad, axis=1, keepdims=True)
    return ((grad - unit * inner) * inv_norm).astype(bf16)


def pair_weights(anchors, candidates, counts, block):
    logits = dot_nt(anchors, candidates)
    terms = jnp.exp(logits * inverse_sharpness - logit_bound)
    parts = []
    for first in range(0, candidates.shape[0], block):
        part = terms[:, first : first + block]
        count = counts[:, first : first + block].astype(f32)
        pairs = jnp.sum(count, axis=1, keepdims=True)
        total = jnp.sum(part, axis=1, keepdims=True)
        parts.append((part * (pairs / total) - count).astype(bf16))
    return jnp.concatenate(parts, axis=1)


def split(runs):
    near = 1 << (runs.bit_length() // 2)
    return near, runs // near


def turn(k):
    return (k & -k).bit_length() - 1


def partners(k, odd, runs):
    pairs = [(i, (i + k) % runs) for i in range(runs) if (i >> turn(k)) % 2 == odd]
    return pairs + [(j, i) for i, j in pairs]


def slot_start(listed, blocks, block, run, runs, reach):
    offset = lax.rem(lax.div(listed, blocks) - run + reach + runs, runs) - reach
    order = 0
    for k in range(1, reach + 1):
        odd = lax.rem(lax.shift_right_logical(run, turn(k)), 2)
        order = jnp.where(offset == k, k + reach * odd, order)
        order = jnp.where(offset == -k, k + reach * (1 - odd), order)
    return (order * blocks + lax.rem(listed, blocks)) * block


def pair_counts(list_ref, live_ref, src_ref, tgt_ref, block, run, runs, reach):
    blocks, slots, pairs = src_ref.shape
    candidates = (2 * reach + 1) * blocks
    point = lax.broadcasted_iota(jnp.int32, (block, pairs), 0)
    place = lax.broadcasted_iota(jnp.int32, (candidates * block, pairs), 0)
    rows = []
    for b in range(blocks):
        left = []
        right = []
        for s in range(slots):
            first = slot_start(list_ref[b, s], blocks, block, run, runs, reach)
            first = jnp.where(s < live_ref[0, b], first, -block)
            key = tgt_ref[b, s : s + 1, :] + first
            left.append(jnp.where(src_ref[b, s : s + 1, :] == point, 1.0, 0.0).astype(bf16))
            right.append(jnp.where(key == place, 1.0, 0.0).astype(bf16))
        rows.append(dot_nt(jnp.concatenate(left, axis=1), jnp.concatenate(right, axis=1)))
    return jnp.concatenate(rows, axis=0)


def load(pairs, sem):
    copies = [pltpu.make_async_copy(src, dst, sem.at[i]) for i, (src, dst) in enumerate(pairs)]
    for copy in copies:
        copy.start()
    return copies


def moment_kernel(
    far, near, scale, run_ref, xs_hbm, xt_hbm, w_hbm, src_hbm, tgt_hbm, *refs
):
    out_refs = refs[:far]
    src_unit_ref, src_inv_ref, tgt_unit_ref, tgt_inv_ref, src_ref, tgt_ref = refs[far : far + 6]
    xs_ref, xt_ref, w_ref, packed_ref, sem = refs[far + 6 :]
    copies = load(
        (
            (w_hbm, w_ref),
            (xs_hbm, xs_ref),
            (xt_hbm, xt_ref),
            (src_hbm, src_ref),
            (tgt_hbm, tgt_ref),
        ),
        sem,
    )
    copies[0].wait()
    copies[1].wait()
    weight = w_ref[...]
    unit, inv_norm = project(xs_ref[...], weight)
    src_unit_ref[...] = unit
    src_inv_ref[...] = jnp.broadcast_to(inv_norm, src_inv_ref.shape)
    zs = unit.astype(bf16)
    copies[2].wait()
    unit, inv_norm = project(xt_ref[...], weight)
    tgt_unit_ref[...] = unit
    tgt_inv_ref[...] = jnp.broadcast_to(inv_norm, tgt_inv_ref.shape)
    zt = unit.astype(bf16)
    moment = (dot_tn(zs, zs) + dot_tn(zt, zt)) * scale
    at = 0
    for r in range(0, moment.shape[0], lane):
        for c in range(r, moment.shape[1], lane):
            packed_ref[at : at + lane, :] = moment[r : r + lane, c : c + lane].astype(bf16)
            at += lane
    if at < packed_ref.shape[0]:
        packed_ref[at:, :] = jnp.zeros((packed_ref.shape[0] - at, lane), bf16)
    rows = packed_ref.shape[0] // far
    place = lax.div(run_ref[0], near)
    for k in range(far):
        first = lax.bitwise_xor(place, k) * rows
        out_refs[k][...] = packed_ref[pl.ds(pl.multiple_of(first, 16), rows), :]
    copies[3].wait()
    copies[4].wait()


def own_kernel(
    runs, reach,
    run_ref, list_ref, live_ref, xt_ref, src_unit_ref, tgt_unit_ref, tgt_inv_ref, src_ref, tgt_ref,
    count_ref, grad_ref, part_ref,
):
    zs = src_unit_ref[...].astype(bf16)
    own = xt_ref.shape[0]
    block = own // src_ref.shape[0]
    counts = pair_counts(
        list_ref, live_ref, src_ref, tgt_ref, block, run_ref[0], runs, reach
    )
    count_ref[...] = counts[:, own:].astype(bf16)
    rows = xt_ref[...]
    grad_ref[...], tgt_grad = score(
        tgt_unit_ref[...], tgt_inv_ref[:, :1], zs, counts[:, :own], block
    )
    part_ref[...] = dot_tn(rows, tgt_grad)


def score(unit, inv_norm, zs, counts, block):
    zt = unit.astype(bf16)
    weights = pair_weights(zs, zt, counts, block)
    grad_zt = dot_tn(weights, zs) * inverse_sharpness
    return dot_nn(weights, zt), back_norm(unit, inv_norm, grad_zt)


def chunk_grad(first, chunk, row_refs, grads, part_ref, total_ref):
    if chunk % lane == 0:
        columns = pl.ds(pl.multiple_of(first, chunk), chunk)
        rows = jnp.concatenate([ref[:, columns] for ref in row_refs], axis=0)
        return part_ref[columns, :] + dot_tn(rows, grads)
    rows = jnp.concatenate([ref[...] for ref in row_refs], axis=0)
    total_ref[...] = part_ref[...] + dot_tn(rows, grads)
    return total_ref[pl.ds(pl.multiple_of(first, chunk), chunk), :]


def halo_kernel(
    block, groups,
    grp_ref, w_ref, unit_ref, inv_ref, count_ref, grad_ref, part_ref, xs_ref, *refs,
):
    send_ref, src_grad_ref, tgt_grad_ref, total_ref = refs[-4:]
    row_refs = refs[:-4]
    rows = jnp.concatenate([ref[...] for ref in row_refs], axis=0)
    unit = unit_ref[...]
    zs = unit.astype(bf16)
    grad, tgt_grad = score(*project(rows, w_ref[...]), zs, count_ref[...], block)
    grad_zs = (grad_ref[...] + grad) * inverse_sharpness
    src_grad = back_norm(unit, inv_ref[:, :1], grad_zs)
    src_grad_ref[...] = src_grad
    tgt_grad_ref[...] = tgt_grad
    grads = jnp.concatenate([src_grad, tgt_grad], axis=0)
    chunk = part_ref.shape[0] // groups
    for k in range(1, groups):
        first = lax.rem(grp_ref[0] + k, groups) * chunk
        send_ref[k - 1] = chunk_grad(
            first, chunk, (xs_ref,) + row_refs, grads, part_ref, total_ref
        ).astype(bf16)


def keep_kernel(grp_ref, part_ref, src_grad_ref, tgt_grad_ref, *refs):
    keep_ref, total_ref = refs[-2:]
    grads = jnp.concatenate([src_grad_ref[...], tgt_grad_ref[...]], axis=0)
    chunk = keep_ref.shape[0]
    keep_ref[...] = chunk_grad(
        grp_ref[0] * chunk, chunk, refs[:-2], grads, part_ref, total_ref
    )


def tree(parts):
    while len(parts) > 1:
        parts = [parts[i] + parts[i + 1] for i in range(0, len(parts), 2)]
    return parts[0]


def deal_kernel(near, groups, run_ref, *refs):
    keep_ref, *got_refs = refs[:groups]
    total_ref, sum_ref = refs[-2:]
    out_refs = refs[-2 - near : -2]
    piece_refs = refs[groups : -2 - near]
    total = keep_ref[...]
    for ref in got_refs:
        total = total + ref[...].astype(f32)
    total_ref[...] = total
    sum_ref[...] = tree([ref[...].astype(f32) for ref in piece_refs]).astype(bf16)
    place = lax.rem(run_ref[0], near)
    rows = total_ref.shape[0] // near
    below = sum_ref.shape[0] // near
    for k in range(near):
        owner = lax.bitwise_xor(place, k)
        part = total_ref[pl.ds(pl.multiple_of(owner * rows, rows), rows), :].astype(bf16)
        at = 0
        for c in range(0, total_ref.shape[1], lane):
            out_refs[k][at : at + rows, :] = part[:, c : c + lane]
            at += rows
        first = pl.multiple_of(owner * below, 16)
        out_refs[k][at : at + below, :] = sum_ref[pl.ds(first, below), :]


def near_kernel(rows, *refs):
    part = tree([ref[...].astype(f32) for ref in refs[:-2]]).astype(bf16)
    refs[-2][...] = part
    refs[-1][...] = part[rows:, :]


def far_kernel(rows, *refs):
    out_ref = refs[-1]
    out_ref[:rows, :] = tree([ref[:rows, :].astype(f32) for ref in refs[:-1]]).astype(bf16)
    below = refs[0].shape[0] - rows
    for i, ref in enumerate(refs[1:-1]):
        at = rows + i * below
        out_ref[at : at + below, :] = ref[rows:, :]


def gather_kernel(rows, *refs):
    out_ref = refs[-1]
    for i, ref in enumerate(refs[:-1]):
        out_ref[i * rows : (i + 1) * rows, :] = ref[:rows, :]


def spread_rows(chunk_ref, half_ref, near, place):
    rows = half_ref.shape[0] // near
    at = 0
    for m in range(near):
        first = pl.multiple_of(lax.bitwise_xor(place, m) * rows, rows)
        for c in range(0, half_ref.shape[1], lane):
            half_ref[pl.ds(first, rows), c : c + lane] = chunk_ref[at : at + rows, :].astype(f32)
            at += rows


def unpack_kernel(near, far, run_ref, grp_ref, half_in_ref, *refs):
    column_refs = refs[:near]
    side_refs = refs[near : 2 * near]
    cov_hbm, grad_hbm, packed_ref, cov_ref, half_ref, sem = refs[2 * near :]
    chunk = half_ref.shape[0]
    spread_rows(half_in_ref, half_ref, near, lax.rem(run_ref[0], near))
    first = pl.multiple_of(grp_ref[0] * chunk, chunk)
    copies = [
        pltpu.make_async_copy(half_ref, grad_hbm.at[pl.ds(first, chunk), :], sem.at[0])
    ]
    copies[0].start()
    rows = packed_ref.shape[0] // (near * far)
    skip = column_refs[0].shape[0] - (far - 1) * rows
    for m, ref in enumerate(column_refs):
        for k in range(far):
            owner = lax.bitwise_xor(run_ref[0], k * near + m)
            at = skip + (k - 1) * rows
            piece = ref[at : at + rows, :] if k else side_refs[m][...]
            packed_ref[pl.ds(pl.multiple_of(owner * rows, 16), rows), :] = piece
    at = 0
    for i, r in enumerate(range(0, cov_ref.shape[0], lane)):
        for c in range(r, cov_ref.shape[1], lane):
            tile = packed_ref[at : at + lane, :].astype(f32)
            cov_ref[r : r + lane, c : c + lane] = tile
            if c > r:
                cov_ref[c : c + lane, r : r + lane] = tile.T
            at += lane
        copy = pltpu.make_async_copy(
            cov_ref.at[r : r + lane, :], cov_hbm.at[r : r + lane, :], sem.at[i + 1]
        )
        copy.start()
        copies.append(copy)
    for copy in copies:
        copy.wait()


def place_kernel(near, run_ref, grp_ref, *refs):
    grad_hbm, chunk_ref, sem = refs[-3:]
    half_refs = refs[:-4]
    groups = len(half_refs) + 1
    chunk = chunk_ref.shape[1]
    copies = []
    for j, ref in enumerate(half_refs):
        spread_rows(ref, chunk_ref.at[j], near, lax.rem(run_ref[0], near))
        first = pl.multiple_of(lax.rem(grp_ref[0] + j + 1, groups) * chunk, chunk)
        copy = pltpu.make_async_copy(
            chunk_ref.at[j], grad_hbm.at[pl.ds(first, chunk), :], sem.at[j]
        )
        copy.start()
        copies.append(copy)
    for copy in copies:
        copy.wait()


def swap(array, bits, runs):
    return lax.ppermute(array, "blk", [(i, i ^ bits) for i in range(runs)])


def small_call(kernel, shapes, specs, scratch=()):
    vmem = pl.BlockSpec(memory_space=pltpu.VMEM)
    many = isinstance(shapes, tuple)
    return pl.pallas_call(
        kernel,
        out_shape=shapes,
        in_specs=specs,
        out_specs=(vmem,) * len(shapes) if many else vmem,
        scratch_shapes=scratch,
        compiler_params=room(16),
    )


def body(src_feats, tgt_feats, proj_weight, match_blocks, match_count, pair_src, pair_tgt):
    xs = src_feats[0]
    xt = tgt_feats[0]
    points, width = xs.shape
    blocks = pair_src.shape[1]
    block = points // blocks
    runs = lax.axis_size("blk")
    groups = lax.axis_size("grp")
    reach = runs // 16
    run = lax.axis_index("blk")
    grp = lax.axis_index("grp")

    hops = range(1, reach + 1)
    odd = [lax.ppermute(xt, "blk", partners(k, 1, runs)) for k in hops]
    even = [lax.ppermute(xt, "blk", partners(k, 0, runs)) for k in hops]

    tiles = width // lane
    near, far = split(runs)
    piece_rows = -(-tiles * (tiles + 1) // 2 * lane // (16 * runs)) * 16
    column_rows = near * piece_rows
    chunk = width // groups
    grad_rows = chunk // near * tiles
    scale = width / (2.0 * points * runs)
    vmem = pl.BlockSpec(memory_space=pltpu.VMEM)
    smem = pl.BlockSpec(memory_space=pltpu.SMEM)
    hbm = pl.BlockSpec(memory_space=pltpu.HBM)
    run_id = run.reshape(1)
    grp_id = grp.reshape(1)

    far_away = [
        pltpu.with_memory_space_constraint(array, pltpu.HBM)
        for array in (xs, xt, proj_weight, pair_src[0], pair_tgt[0])
    ]
    *pieces, unit, inv, tgt_unit, tgt_inv, sources, targets = pl.pallas_call(
        functools.partial(moment_kernel, far, near, scale),
        out_shape=(jax.ShapeDtypeStruct((column_rows, lane), bf16),) * far
        + (jax.ShapeDtypeStruct((points, width), f32), jax.ShapeDtypeStruct((points, lane), f32))
        * 2
        + (jax.ShapeDtypeStruct(pair_src.shape[1:], jnp.int32),) * 2,
        in_specs=[smem] + [hbm] * 5,
        out_specs=(vmem,) * (far + 6),
        scratch_shapes=[
            pltpu.VMEM((points, width), bf16),
            pltpu.VMEM((points, width), bf16),
            pltpu.VMEM((width, width), bf16),
            pltpu.VMEM((far * column_rows, lane), bf16),
            pltpu.SemaphoreType.DMA((5,)),
        ],
        compiler_params=room(16),
        name="moment",
    )(run_id, *far_away)
    pieces = [pieces[0]] + [swap(pieces[k], k * near, runs) for k in range(1, far)]
    counts, grad, part = pl.pallas_call(
        functools.partial(own_kernel, runs, reach),
        out_shape=(
            jax.ShapeDtypeStruct((points, 2 * reach * points), bf16),
            jax.ShapeDtypeStruct((points, width), f32),
            jax.ShapeDtypeStruct((width, width), f32),
        ),
        in_specs=[smem] * 3 + [vmem] * 6,
        out_specs=(vmem,) * 3,
        compiler_params=room(16 + 4 * reach),
        name="own",
    )(
        run_id, match_blocks[0], match_count, xt, unit, tgt_unit, tgt_inv, sources, targets
    )
    total = [pltpu.VMEM((width, width), f32)]
    send, src_grad, tgt_grad = pl.pallas_call(
        functools.partial(halo_kernel, block, groups),
        out_shape=(
            jax.ShapeDtypeStruct((groups - 1, chunk, width), bf16),
            jax.ShapeDtypeStruct((points, width), bf16),
            jax.ShapeDtypeStruct((2 * reach * points, width), bf16),
        ),
        in_specs=[smem] + [vmem] * (7 + 2 * reach),
        out_specs=(vmem,) * 3,
        scratch_shapes=total,
        compiler_params=room(16 + 4 * reach),
        name="halo",
    )(grp_id, proj_weight, unit, inv, counts, grad, part, xs, *even, *odd)
    got = [
        lax.ppermute(send[k - 1], "grp", [(i, (i + k) % groups) for i in range(groups)])
        for k in range(1, groups)
    ]
    keep = small_call(
        keep_kernel,
        jax.ShapeDtypeStruct((chunk, width), f32),
        [smem] + [vmem] * (4 + 2 * reach),
        total,
    )(grp_id, part, src_grad, tgt_grad, xs, *even, *odd)
    part_shape = jax.ShapeDtypeStruct((grad_rows + piece_rows, lane), bf16)
    parts = small_call(
        functools.partial(deal_kernel, near, groups),
        (part_shape,) * near,
        [smem] + [vmem] * (groups + far),
        [pltpu.VMEM((chunk, width), f32), pltpu.VMEM((column_rows, lane), bf16)],
    )(run_id, keep, *got, *pieces)
    parts = [parts[0]] + [swap(parts[k], k, runs) for k in range(1, near)]
    part, piece = small_call(
        functools.partial(near_kernel, grad_rows),
        (part_shape, jax.ShapeDtypeStruct((piece_rows, lane), bf16)),
        [vmem] * near,
    )(*parts)
    parts = [part] + [swap(part, k * near, runs) for k in range(1, far)]
    sides = [piece] + [swap(piece, k, runs) for k in range(1, near)]
    part = small_call(
        functools.partial(far_kernel, grad_rows),
        jax.ShapeDtypeStruct((grad_rows + (far - 1) * piece_rows, lane), bf16),
        [vmem] * far,
    )(*parts)
    columns = [part] + [swap(part, k, runs) for k in range(1, near)]
    half = small_call(
        functools.partial(gather_kernel, grad_rows),
        jax.ShapeDtypeStruct((near * grad_rows, lane), bf16),
        [vmem] * near,
    )(*columns)
    halves = [half] + [
        lax.ppermute(half, "grp", [(i, (i - k) % groups) for i in range(groups)])
        for k in range(1, groups)
    ]
    square = jax.ShapeDtypeStruct((width, width), f32)
    covariance, own_rows = pl.pallas_call(
        functools.partial(unpack_kernel, near, far),
        out_shape=(square, square),
        in_specs=[smem] * 2 + [vmem] * (1 + 2 * near),
        out_specs=(hbm, hbm),
        scratch_shapes=[
            pltpu.VMEM((far * column_rows, lane), bf16),
            pltpu.VMEM((width, width), f32),
            pltpu.VMEM((chunk, width), f32),
            pltpu.SemaphoreType.DMA((1 + tiles,)),
        ],
        compiler_params=room(16),
        name="unpack",
    )(run_id, grp_id, half, *columns, *sides)
    weight_grad = pl.pallas_call(
        functools.partial(place_kernel, near),
        out_shape=square,
        in_specs=[smem] * 2 + [vmem] * (groups - 1) + [hbm],
        out_specs=hbm,
        scratch_shapes=[
            pltpu.VMEM((groups - 1, chunk, width), f32),
            pltpu.SemaphoreType.DMA((groups - 1,)),
        ],
        input_output_aliases={1 + groups: 0},
        compiler_params=room(16),
        name="place",
    )(run_id, grp_id, *halves[1:], own_rows)
    return (weight_grad, covariance[None])


def solution(mesh):
    placed = (
        P("grp", "blk", None),
        P("grp", "blk", None),
        P(),
        P("grp", "blk", None),
        P("grp", "blk"),
        P("grp", "blk", None, None),
        P("grp", "blk", None, None),
    )
    return jax.shard_map(
        body, mesh=mesh, in_specs=placed, out_specs=(P(), P("grp", None, None)), check_vma=False
    )
```

```python
import functools
import jax
import jax.numpy as jnp
from jax import lax
from jax.experimental import pallas as pl
from jax.experimental.pallas import tpu as pltpu
from jax.sharding import PartitionSpec as P


inverse_sharpness = 2.5
logit_bound = 2.5
norm_eps = 1e-06
lane = 128


f32 = jnp.float32
bf16 = jnp.bfloat16


def dot_nn(a, b):
    return lax.dot_general(a, b, (((1,), (0,)), ((), ())), preferred_element_type=f32)


def dot_nt(a, b):
    return lax.dot_general(a, b, (((1,), (1,)), ((), ())), preferred_element_type=f32)


def dot_tn(a, b):
    return lax.dot_general(a, b, (((0,), (0,)), ((), ())), preferred_element_type=f32)


def room(mebibytes):
    return pltpu.CompilerParams(vmem_limit_bytes=mebibytes * 1024 * 1024)


def project(rows, weight):
    projected = dot_nn(rows, weight)
    inv_norm = lax.rsqrt(jnp.sum(projected * projected, axis=1, keepdims=True) + norm_eps)
    return projected * inv_norm, inv_norm


def back_norm(unit, inv_norm, grad):
    inner = jnp.sum(unit * grad, axis=1, keepdims=True)
    return ((grad - unit * inner) * inv_norm).astype(bf16)


def pair_weights(anchors, candidates, counts, block):
    logits = dot_nt(anchors, candidates)
    terms = jnp.exp(logits * inverse_sharpness - logit_bound)
    parts = []
    for first in range(0, candidates.shape[0], block):
        part = terms[:, first : first + block]
        count = counts[:, first : first + block].astype(f32)
        pairs = jnp.sum(count, axis=1, keepdims=True)
        total = jnp.sum(part, axis=1, keepdims=True)
        parts.append((part * (pairs / total) - count).astype(bf16))
    return jnp.concatenate(parts, axis=1)


def split(runs):
    near = 1 << (runs.bit_length() // 2)
    return near, runs // near


def turn(k):
    return (k & -k).bit_length() - 1


def partners(k, odd, runs):
    pairs = [(i, (i + k) % runs) for i in range(runs) if (i >> turn(k)) % 2 == odd]
    return pairs + [(j, i) for i, j in pairs]


def slot_start(listed, blocks, block, run, runs, reach):
    offset = lax.rem(lax.div(listed, blocks) - run + reach + runs, runs) - reach
    order = 0
    for k in range(1, reach + 1):
        odd = lax.rem(lax.shift_right_logical(run, turn(k)), 2)
        order = jnp.where(offset == k, k + reach * odd, order)
        order = jnp.where(offset == -k, k + reach * (1 - odd), order)
    return (order * blocks + lax.rem(listed, blocks)) * block


def pair_counts(list_ref, live_ref, src_ref, tgt_ref, count_ref, block, run, runs, reach):
    blocks, slots, pairs = src_ref.shape
    spare = (2 * reach + 1) * blocks * block
    point = lax.broadcasted_iota(jnp.int32, (block, pairs), 0)
    count_ref[...] = jnp.zeros_like(count_ref)
    for b in range(blocks):
        for s in range(slots):
            first = slot_start(list_ref[b, s], blocks, block, run, runs, reach)
            first = jnp.where(s < live_ref[0, b], first, spare)
            left = jnp.where(src_ref[b, s : s + 1, :] == point, 1.0, 0.0).astype(bf16)
            right = jnp.where(tgt_ref[b, s : s + 1, :] == point, 1.0, 0.0).astype(bf16)
            place = (slice(b * block, (b + 1) * block), pl.ds(pl.multiple_of(first, block), block))
            count_ref[place] = count_ref[place] + dot_nt(left, right)


def load(pairs, sem):
    copies = [pltpu.make_async_copy(src, dst, sem.at[i]) for i, (src, dst) in enumerate(pairs)]
    for copy in copies:
        copy.start()
    return copies


def moment_kernel(
    far, near, scale, run_ref, xs_hbm, xt_hbm, w_hbm, src_hbm, tgt_hbm, *refs
):
    out_refs = refs[:far]
    src_unit_ref, src_inv_ref, tgt_unit_ref, tgt_inv_ref, src_ref, tgt_ref = refs[far : far + 6]
    xs_ref, xt_ref, w_ref, packed_ref, sem = refs[far + 6 :]
    copies = load(
        (
            (w_hbm, w_ref),
            (xs_hbm, xs_ref),
            (xt_hbm, xt_ref),
            (src_hbm, src_ref),
            (tgt_hbm, tgt_ref),
        ),
        sem,
    )
    copies[0].wait()
    copies[1].wait()
    weight = w_ref[...]
    unit, inv_norm = project(xs_ref[...], weight)
    src_unit_ref[...] = unit
    src_inv_ref[...] = jnp.broadcast_to(inv_norm, src_inv_ref.shape)
    zs = unit.astype(bf16)
    copies[2].wait()
    unit, inv_norm = project(xt_ref[...], weight)
    tgt_unit_ref[...] = unit
    tgt_inv_ref[...] = jnp.broadcast_to(inv_norm, tgt_inv_ref.shape)
    zt = unit.astype(bf16)
    moment = (dot_tn(zs, zs) + dot_tn(zt, zt)) * scale
    at = 0
    for r in range(0, moment.shape[0], lane):
        for c in range(r, moment.shape[1], lane):
            packed_ref[at : at + lane, :] = moment[r : r + lane, c : c + lane].astype(bf16)
            at += lane
    if at < packed_ref.shape[0]:
        packed_ref[at:, :] = jnp.zeros((packed_ref.shape[0] - at, lane), bf16)
    rows = packed_ref.shape[0] // far
    place = lax.div(run_ref[0], near)
    for k in range(far):
        first = lax.bitwise_xor(place, k) * rows
        out_refs[k][...] = packed_ref[pl.ds(pl.multiple_of(first, 16), rows), :]
    copies[3].wait()
    copies[4].wait()


def own_kernel(
    runs, reach,
    run_ref, list_ref, live_ref, xt_ref, src_unit_ref, tgt_unit_ref, tgt_inv_ref, src_ref, tgt_ref,
    count_ref, grad_ref, part_ref, all_ref,
):
    zs = src_unit_ref[...].astype(bf16)
    own = xt_ref.shape[0]
    block = own // src_ref.shape[0]
    pair_counts(
        list_ref, live_ref, src_ref, tgt_ref, all_ref, block, run_ref[0], runs, reach
    )
    count_ref[...] = all_ref[:, own : own * (2 * reach + 1)].astype(bf16)
    rows = xt_ref[...]
    grad_ref[...], tgt_grad = score(
        tgt_unit_ref[...], tgt_inv_ref[:, :1], zs, all_ref[:, :own], block
    )
    part_ref[...] = dot_tn(rows, tgt_grad)


def score(unit, inv_norm, zs, counts, block):
    zt = unit.astype(bf16)
    weights = pair_weights(zs, zt, counts, block)
    grad_zt = dot_tn(weights, zs) * inverse_sharpness
    return dot_nn(weights, zt), back_norm(unit, inv_norm, grad_zt)


def chunk_grad(first, chunk, row_refs, grads, part_ref, total_ref):
    if chunk % lane == 0:
        columns = pl.ds(pl.multiple_of(first, chunk), chunk)
        rows = jnp.concatenate([ref[:, columns] for ref in row_refs], axis=0)
        return part_ref[columns, :] + dot_tn(rows, grads)
    rows = jnp.concatenate([ref[...] for ref in row_refs], axis=0)
    total_ref[...] = part_ref[...] + dot_tn(rows, grads)
    return total_ref[pl.ds(pl.multiple_of(first, chunk), chunk), :]


def halo_kernel(
    block, groups,
    grp_ref, w_ref, unit_ref, inv_ref, count_ref, grad_ref, part_ref, xs_ref, *refs,
):
    send_ref, src_grad_ref, tgt_grad_ref, total_ref = refs[-4:]
    row_refs = refs[:-4]
    rows = jnp.concatenate([ref[...] for ref in row_refs], axis=0)
    unit = unit_ref[...]
    zs = unit.astype(bf16)
    grad, tgt_grad = score(*project(rows, w_ref[...]), zs, count_ref[...], block)
    grad_zs = (grad_ref[...] + grad) * inverse_sharpness
    src_grad = back_norm(unit, inv_ref[:, :1], grad_zs)
    src_grad_ref[...] = src_grad
    tgt_grad_ref[...] = tgt_grad
    grads = jnp.concatenate([src_grad, tgt_grad], axis=0)
    chunk = part_ref.shape[0] // groups
    for k in range(1, groups):
        first = lax.rem(grp_ref[0] + k, groups) * chunk
        send_ref[k - 1] = chunk_grad(
            first, chunk, (xs_ref,) + row_refs, grads, part_ref, total_ref
        ).astype(bf16)


def keep_kernel(grp_ref, part_ref, src_grad_ref, tgt_grad_ref, *refs):
    keep_ref, total_ref = refs[-2:]
    grads = jnp.concatenate([src_grad_ref[...], tgt_grad_ref[...]], axis=0)
    chunk = keep_ref.shape[0]
    keep_ref[...] = chunk_grad(
        grp_ref[0] * chunk, chunk, refs[:-2], grads, part_ref, total_ref
    )


def tree(parts):
    while len(parts) > 1:
        parts = [parts[i] + parts[i + 1] for i in range(0, len(parts), 2)]
    return parts[0]


def deal_kernel(near, groups, run_ref, *refs):
    keep_ref, *got_refs = refs[:groups]
    total_ref, sum_ref = refs[-2:]
    out_refs = refs[-2 - near : -2]
    piece_refs = refs[groups : -2 - near]
    total = keep_ref[...]
    for ref in got_refs:
        total = total + ref[...].astype(f32)
    total_ref[...] = total
    sum_ref[...] = tree([ref[...].astype(f32) for ref in piece_refs]).astype(bf16)
    place = lax.rem(run_ref[0], near)
    rows = total_ref.shape[0] // near
    below = sum_ref.shape[0] // near
    for k in range(near):
        owner = lax.bitwise_xor(place, k)
        part = total_ref[pl.ds(pl.multiple_of(owner * rows, rows), rows), :].astype(bf16)
        at = 0
        for c in range(0, total_ref.shape[1], lane):
            out_refs[k][at : at + rows, :] = part[:, c : c + lane]
            at += rows
        first = pl.multiple_of(owner * below, 16)
        out_refs[k][at : at + below, :] = sum_ref[pl.ds(first, below), :]


def near_kernel(rows, *refs):
    part = tree([ref[...].astype(f32) for ref in refs[:-2]]).astype(bf16)
    refs[-2][...] = part
    refs[-1][...] = part[rows:, :]


def far_kernel(rows, *refs):
    out_ref = refs[-1]
    out_ref[:rows, :] = tree([ref[:rows, :].astype(f32) for ref in refs[:-1]]).astype(bf16)
    below = refs[0].shape[0] - rows
    for i, ref in enumerate(refs[1:-1]):
        at = rows + i * below
        out_ref[at : at + below, :] = ref[rows:, :]


def gather_kernel(rows, *refs):
    out_ref = refs[-1]
    for i, ref in enumerate(refs[:-1]):
        out_ref[i * rows : (i + 1) * rows, :] = ref[:rows, :]


def spread_rows(chunk_ref, half_ref, near, place):
    rows = half_ref.shape[0] // near
    at = 0
    for m in range(near):
        first = pl.multiple_of(lax.bitwise_xor(place, m) * rows, rows)
        for c in range(0, half_ref.shape[1], lane):
            half_ref[pl.ds(first, rows), c : c + lane] = chunk_ref[at : at + rows, :].astype(f32)
            at += rows


def unpack_kernel(near, far, run_ref, grp_ref, half_in_ref, *refs):
    column_refs = refs[:near]
    side_refs = refs[near : 2 * near]
    cov_hbm, grad_hbm, packed_ref, cov_ref, half_ref, sem = refs[2 * near :]
    chunk = half_ref.shape[0]
    spread_rows(half_in_ref, half_ref, near, lax.rem(run_ref[0], near))
    first = pl.multiple_of(grp_ref[0] * chunk, chunk)
    copies = [
        pltpu.make_async_copy(half_ref, grad_hbm.at[pl.ds(first, chunk), :], sem.at[0])
    ]
    copies[0].start()
    rows = packed_ref.shape[0] // (near * far)
    skip = column_refs[0].shape[0] - (far - 1) * rows
    for m, ref in enumerate(column_refs):
        for k in range(far):
            owner = lax.bitwise_xor(run_ref[0], k * near + m)
            at = skip + (k - 1) * rows
            piece = ref[at : at + rows, :] if k else side_refs[m][...]
            packed_ref[pl.ds(pl.multiple_of(owner * rows, 16), rows), :] = piece
    at = 0
    for i, r in enumerate(range(0, cov_ref.shape[0], lane)):
        for c in range(r, cov_ref.shape[1], lane):
            tile = packed_ref[at : at + lane, :].astype(f32)
            cov_ref[r : r + lane, c : c + lane] = tile
            if c > r:
                cov_ref[c : c + lane, r : r + lane] = tile.T
            at += lane
        copy = pltpu.make_async_copy(
            cov_ref.at[r : r + lane, :], cov_hbm.at[r : r + lane, :], sem.at[i + 1]
        )
        copy.start()
        copies.append(copy)
    for copy in copies:
        copy.wait()


def place_kernel(near, run_ref, grp_ref, *refs):
    grad_hbm, chunk_ref, sem = refs[-3:]
    half_refs = refs[:-4]
    groups = len(half_refs) + 1
    chunk = chunk_ref.shape[1]
    copies = []
    for j, ref in enumerate(half_refs):
        spread_rows(ref, chunk_ref.at[j], near, lax.rem(run_ref[0], near))
        first = pl.multiple_of(lax.rem(grp_ref[0] + j + 1, groups) * chunk, chunk)
        copy = pltpu.make_async_copy(
            chunk_ref.at[j], grad_hbm.at[pl.ds(first, chunk), :], sem.at[j]
        )
        copy.start()
        copies.append(copy)
    for copy in copies:
        copy.wait()


def swap(array, bits, runs):
    return lax.ppermute(array, "blk", [(i, i ^ bits) for i in range(runs)])


def small_call(kernel, shapes, specs, scratch=()):
    vmem = pl.BlockSpec(memory_space=pltpu.VMEM)
    many = isinstance(shapes, tuple)
    return pl.pallas_call(
        kernel,
        out_shape=shapes,
        in_specs=specs,
        out_specs=(vmem,) * len(shapes) if many else vmem,
        scratch_shapes=scratch,
        compiler_params=room(16),
    )


def body(src_feats, tgt_feats, proj_weight, match_blocks, match_count, pair_src, pair_tgt):
    xs = src_feats[0]
    xt = tgt_feats[0]
    points, width = xs.shape
    blocks = pair_src.shape[1]
    block = points // blocks
    runs = lax.axis_size("blk")
    groups = lax.axis_size("grp")
    reach = runs // 16
    run = lax.axis_index("blk")
    grp = lax.axis_index("grp")

    hops = range(1, reach + 1)
    odd = [lax.ppermute(xt, "blk", partners(k, 1, runs)) for k in hops]
    even = [lax.ppermute(xt, "blk", partners(k, 0, runs)) for k in hops]

    tiles = width // lane
    near, far = split(runs)
    piece_rows = -(-tiles * (tiles + 1) // 2 * lane // (16 * runs)) * 16
    column_rows = near * piece_rows
    chunk = width // groups
    grad_rows = chunk // near * tiles
    scale = width / (2.0 * points * runs)
    vmem = pl.BlockSpec(memory_space=pltpu.VMEM)
    smem = pl.BlockSpec(memory_space=pltpu.SMEM)
    hbm = pl.BlockSpec(memory_space=pltpu.HBM)
    run_id = run.reshape(1)
    grp_id = grp.reshape(1)

    far_away = [
        pltpu.with_memory_space_constraint(array, pltpu.HBM)
        for array in (xs, xt, proj_weight, pair_src[0], pair_tgt[0])
    ]
    *pieces, unit, inv, tgt_unit, tgt_inv, sources, targets = pl.pallas_call(
        functools.partial(moment_kernel, far, near, scale),
        out_shape=(jax.ShapeDtypeStruct((column_rows, lane), bf16),) * far
        + (jax.ShapeDtypeStruct((points, width), f32), jax.ShapeDtypeStruct((points, lane), f32))
        * 2
        + (jax.ShapeDtypeStruct(pair_src.shape[1:], jnp.int32),) * 2,
        in_specs=[smem] + [hbm] * 5,
        out_specs=(vmem,) * (far + 6),
        scratch_shapes=[
            pltpu.VMEM((points, width), bf16),
            pltpu.VMEM((points, width), bf16),
            pltpu.VMEM((width, width), bf16),
            pltpu.VMEM((far * column_rows, lane), bf16),
            pltpu.SemaphoreType.DMA((5,)),
        ],
        compiler_params=room(16),
        name="moment",
    )(run_id, *far_away)
    pieces = [pieces[0]] + [swap(pieces[k], k * near, runs) for k in range(1, far)]
    counts, grad, part = pl.pallas_call(
        functools.partial(own_kernel, runs, reach),
        out_shape=(
            jax.ShapeDtypeStruct((points, 2 * reach * points), bf16),
            jax.ShapeDtypeStruct((points, width), f32),
            jax.ShapeDtypeStruct((width, width), f32),
        ),
        in_specs=[smem] * 3 + [vmem] * 6,
        out_specs=(vmem,) * 3,
        scratch_shapes=[pltpu.VMEM((points, (2 * reach + 1) * points + block), f32)],
        compiler_params=room(16 + 4 * reach),
        name="own",
    )(
        run_id, match_blocks[0], match_count, xt, unit, tgt_unit, tgt_inv, sources, targets
    )
    total = [pltpu.VMEM((width, width), f32)]
    send, src_grad, tgt_grad = pl.pallas_call(
        functools.partial(halo_kernel, block, groups),
        out_shape=(
            jax.ShapeDtypeStruct((groups - 1, chunk, width), bf16),
            jax.ShapeDtypeStruct((points, width), bf16),
            jax.ShapeDtypeStruct((2 * reach * points, width), bf16),
        ),
        in_specs=[smem] + [vmem] * (7 + 2 * reach),
        out_specs=(vmem,) * 3,
        scratch_shapes=total,
        compiler_params=room(16 + 4 * reach),
        name="halo",
    )(grp_id, proj_weight, unit, inv, counts, grad, part, xs, *even, *odd)
    got = [
        lax.ppermute(send[k - 1], "grp", [(i, (i + k) % groups) for i in range(groups)])
        for k in range(1, groups)
    ]
    keep = small_call(
        keep_kernel,
        jax.ShapeDtypeStruct((chunk, width), f32),
        [smem] + [vmem] * (4 + 2 * reach),
        total,
    )(grp_id, part, src_grad, tgt_grad, xs, *even, *odd)
    part_shape = jax.ShapeDtypeStruct((grad_rows + piece_rows, lane), bf16)
    parts = small_call(
        functools.partial(deal_kernel, near, groups),
        (part_shape,) * near,
        [smem] + [vmem] * (groups + far),
        [pltpu.VMEM((chunk, width), f32), pltpu.VMEM((column_rows, lane), bf16)],
    )(run_id, keep, *got, *pieces)
    parts = [parts[0]] + [swap(parts[k], k, runs) for k in range(1, near)]
    part, piece = small_call(
        functools.partial(near_kernel, grad_rows),
        (part_shape, jax.ShapeDtypeStruct((piece_rows, lane), bf16)),
        [vmem] * near,
    )(*parts)
    parts = [part] + [swap(part, k * near, runs) for k in range(1, far)]
    sides = [piece] + [swap(piece, k, runs) for k in range(1, near)]
    part = small_call(
        functools.partial(far_kernel, grad_rows),
        jax.ShapeDtypeStruct((grad_rows + (far - 1) * piece_rows, lane), bf16),
        [vmem] * far,
    )(*parts)
    columns = [part] + [swap(part, k, runs) for k in range(1, near)]
    half = small_call(
        functools.partial(gather_kernel, grad_rows),
        jax.ShapeDtypeStruct((near * grad_rows, lane), bf16),
        [vmem] * near,
    )(*columns)
    halves = [half] + [
        lax.ppermute(half, "grp", [(i, (i - k) % groups) for i in range(groups)])
        for k in range(1, groups)
    ]
    square = jax.ShapeDtypeStruct((width, width), f32)
    covariance, own_rows = pl.pallas_call(
        functools.partial(unpack_kernel, near, far),
        out_shape=(square, square),
        in_specs=[smem] * 2 + [vmem] * (1 + 2 * near),
        out_specs=(hbm, hbm),
        scratch_shapes=[
            pltpu.VMEM((far * column_rows, lane), bf16),
            pltpu.VMEM((width, width), f32),
            pltpu.VMEM((chunk, width), f32),
            pltpu.SemaphoreType.DMA((1 + tiles,)),
        ],
        compiler_params=room(16),
        name="unpack",
    )(run_id, grp_id, half, *columns, *sides)
    weight_grad = pl.pallas_call(
        functools.partial(place_kernel, near),
        out_shape=square,
        in_specs=[smem] * 2 + [vmem] * (groups - 1) + [hbm],
        out_specs=hbm,
        scratch_shapes=[
            pltpu.VMEM((groups - 1, chunk, width), f32),
            pltpu.SemaphoreType.DMA((groups - 1,)),
        ],
        input_output_aliases={1 + groups: 0},
        compiler_params=room(16),
        name="place",
    )(run_id, grp_id, *halves[1:], own_rows)
    return (weight_grad, covariance[None])


def solution(mesh):
    placed = (
        P("grp", "blk", None),
        P("grp", "blk", None),
        P(),
        P("grp", "blk", None),
        P("grp", "blk"),
        P("grp", "blk", None, None),
        P("grp", "blk", None, None),
    )
    return jax.shard_map(
        body, mesh=mesh, in_specs=placed, out_specs=(P(), P("grp", None, None)), check_vma=False
    )
```

```python
import functools
import jax
import jax.numpy as jnp
from jax import lax
from jax.experimental import pallas as pl
from jax.experimental.pallas import tpu as pltpu
from jax.sharding import PartitionSpec as P


inverse_sharpness = 2.5
logit_bound = 2.5
norm_eps = 1e-06
lane = 128


f32 = jnp.float32
bf16 = jnp.bfloat16


def dot_nn(a, b):
    return lax.dot_general(a, b, (((1,), (0,)), ((), ())), preferred_element_type=f32)


def dot_nt(a, b):
    return lax.dot_general(a, b, (((1,), (1,)), ((), ())), preferred_element_type=f32)


def dot_tn(a, b):
    return lax.dot_general(a, b, (((0,), (0,)), ((), ())), preferred_element_type=f32)


def room(mebibytes):
    return pltpu.CompilerParams(vmem_limit_bytes=mebibytes * 1024 * 1024)


def project(rows, weight):
    projected = dot_nn(rows, weight)
    inv_norm = lax.rsqrt(jnp.sum(projected * projected, axis=1, keepdims=True) + norm_eps)
    return projected * inv_norm, inv_norm


def back_norm(unit, inv_norm, grad):
    inner = jnp.sum(unit * grad, axis=1, keepdims=True)
    return ((grad - unit * inner) * inv_norm).astype(bf16)


def pair_weights(anchors, candidates, counts, block):
    logits = dot_nt(anchors, candidates)
    terms = jnp.exp(logits * inverse_sharpness - logit_bound)
    parts = []
    for first in range(0, candidates.shape[0], block):
        part = terms[:, first : first + block]
        count = counts[:, first : first + block].astype(f32)
        pairs = jnp.sum(count, axis=1, keepdims=True)
        total = jnp.sum(part, axis=1, keepdims=True)
        parts.append((part * (pairs / total) - count).astype(bf16))
    return jnp.concatenate(parts, axis=1)


def split(runs):
    near = 1 << (runs.bit_length() // 2)
    return near, runs // near


def turn(k):
    return (k & -k).bit_length() - 1


def partners(k, odd, runs):
    pairs = [(i, (i + k) % runs) for i in range(runs) if (i >> turn(k)) % 2 == odd]
    return pairs + [(j, i) for i, j in pairs]


def slot_start(listed, blocks, block, run, runs, reach):
    offset = lax.rem(lax.div(listed, blocks) - run + reach + runs, runs) - reach
    order = 0
    for k in range(1, reach + 1):
        odd = lax.rem(lax.shift_right_logical(run, turn(k)), 2)
        order = jnp.where(offset == k, k + reach * odd, order)
        order = jnp.where(offset == -k, k + reach * (1 - odd), order)
    return (order * blocks + lax.rem(listed, blocks)) * block


def pair_counts(list_ref, live_ref, src_ref, tgt_ref, count_ref, block, run, runs, reach):
    blocks, slots, pairs = src_ref.shape
    spare = (2 * reach + 1) * blocks * block
    point = lax.broadcasted_iota(jnp.int32, (block, pairs), 0)
    count_ref[...] = jnp.zeros_like(count_ref)
    for b in range(blocks):
        for s in range(slots):
            first = slot_start(list_ref[b, s], blocks, block, run, runs, reach)
            first = jnp.where(s < live_ref[0, b], first, spare)
            left = jnp.where(src_ref[b, s : s + 1, :] == point, 1.0, 0.0).astype(bf16)
            right = jnp.where(tgt_ref[b, s : s + 1, :] == point, 1.0, 0.0).astype(bf16)
            place = (slice(b * block, (b + 1) * block), pl.ds(pl.multiple_of(first, block), block))
            count_ref[place] = count_ref[place] + dot_nt(left, right)


def load(pairs, sem):
    copies = [pltpu.make_async_copy(src, dst, sem.at[i]) for i, (src, dst) in enumerate(pairs)]
    for copy in copies:
        copy.start()
    return copies


def moment_kernel(
    far, near, scale, run_ref, xs_hbm, xt_hbm, w_hbm, src_hbm, tgt_hbm, *refs
):
    out_refs = refs[:far]
    src_unit_ref, src_inv_ref, tgt_unit_ref, tgt_inv_ref, src_ref, tgt_ref = refs[far : far + 6]
    xs_ref, xt_ref, w_ref, packed_ref, sem = refs[far + 6 :]
    copies = load(
        (
            (w_hbm, w_ref),
            (xs_hbm, xs_ref),
            (xt_hbm, xt_ref),
            (src_hbm, src_ref),
            (tgt_hbm, tgt_ref),
        ),
        sem,
    )
    copies[0].wait()
    copies[1].wait()
    weight = w_ref[...]
    unit, inv_norm = project(xs_ref[...], weight)
    src_unit_ref[...] = unit
    src_inv_ref[...] = jnp.broadcast_to(inv_norm, src_inv_ref.shape)
    zs = unit.astype(bf16)
    copies[2].wait()
    unit, inv_norm = project(xt_ref[...], weight)
    tgt_unit_ref[...] = unit
    tgt_inv_ref[...] = jnp.broadcast_to(inv_norm, tgt_inv_ref.shape)
    zt = unit.astype(bf16)
    moment = (dot_tn(zs, zs) + dot_tn(zt, zt)) * scale
    at = 0
    for r in range(0, moment.shape[0], lane):
        for c in range(r, moment.shape[1], lane):
            packed_ref[at : at + lane, :] = moment[r : r + lane, c : c + lane].astype(bf16)
            at += lane
    if at < packed_ref.shape[0]:
        packed_ref[at:, :] = jnp.zeros((packed_ref.shape[0] - at, lane), bf16)
    rows = packed_ref.shape[0] // far
    place = lax.div(run_ref[0], near)
    for k in range(far):
        first = lax.bitwise_xor(place, k) * rows
        out_refs[k][...] = packed_ref[pl.ds(pl.multiple_of(first, 16), rows), :]
    copies[3].wait()
    copies[4].wait()


def own_kernel(
    runs, reach,
    run_ref, list_ref, live_ref, xt_ref, src_unit_ref, tgt_unit_ref, tgt_inv_ref, src_ref, tgt_ref,
    count_ref, grad_ref, part_ref, all_ref,
):
    zs = src_unit_ref[...].astype(bf16)
    own = xt_ref.shape[0]
    block = own // src_ref.shape[0]
    pair_counts(
        list_ref, live_ref, src_ref, tgt_ref, all_ref, block, run_ref[0], runs, reach
    )
    count_ref[...] = all_ref[:, own : own * (2 * reach + 1)].astype(bf16)
    rows = xt_ref[...]
    grad_ref[...], tgt_grad = score(
        tgt_unit_ref[...], tgt_inv_ref[:, :1], zs, all_ref[:, :own], block
    )
    part_ref[...] = dot_tn(rows, tgt_grad)


def score(unit, inv_norm, zs, counts, block):
    zt = unit.astype(bf16)
    weights = pair_weights(zs, zt, counts, block)
    grad_zt = dot_tn(weights, zs) * inverse_sharpness
    return dot_nn(weights, zt), back_norm(unit, inv_norm, grad_zt)


def chunk_grad(first, chunk, row_refs, grads, part_ref, total_ref):
    if chunk % lane == 0:
        columns = pl.ds(pl.multiple_of(first, chunk), chunk)
        rows = jnp.concatenate([ref[:, columns] for ref in row_refs], axis=0)
        return part_ref[columns, :] + dot_tn(rows, grads)
    rows = jnp.concatenate([ref[...] for ref in row_refs], axis=0)
    total_ref[...] = part_ref[...] + dot_tn(rows, grads)
    return total_ref[pl.ds(pl.multiple_of(first, chunk), chunk), :]


def halo_kernel(
    block, groups,
    grp_ref, w_ref, unit_ref, inv_ref, count_ref, grad_ref, part_ref, xs_ref, *refs,
):
    send_ref, src_grad_ref, tgt_grad_ref, total_ref = refs[-4:]
    row_refs = refs[:-4]
    rows = jnp.concatenate([ref[...] for ref in row_refs], axis=0)
    unit = unit_ref[...]
    zs = unit.astype(bf16)
    grad, tgt_grad = score(*project(rows, w_ref[...]), zs, count_ref[...], block)
    grad_zs = (grad_ref[...] + grad) * inverse_sharpness
    src_grad = back_norm(unit, inv_ref[:, :1], grad_zs)
    src_grad_ref[...] = src_grad
    tgt_grad_ref[...] = tgt_grad
    grads = jnp.concatenate([src_grad, tgt_grad], axis=0)
    chunk = part_ref.shape[0] // groups
    for k in range(1, groups):
        first = lax.rem(grp_ref[0] + k, groups) * chunk
        send_ref[k - 1] = chunk_grad(
            first, chunk, (xs_ref,) + row_refs, grads, part_ref, total_ref
        ).astype(bf16)


def keep_kernel(grp_ref, part_ref, src_grad_ref, tgt_grad_ref, *refs):
    keep_ref, total_ref = refs[-2:]
    grads = jnp.concatenate([src_grad_ref[...], tgt_grad_ref[...]], axis=0)
    chunk = keep_ref.shape[0]
    keep_ref[...] = chunk_grad(
        grp_ref[0] * chunk, chunk, refs[:-2], grads, part_ref, total_ref
    )


def tree(parts):
    while len(parts) > 1:
        parts = [parts[i] + parts[i + 1] for i in range(0, len(parts), 2)]
    return parts[0]


def deal_kernel(near, groups, run_ref, *refs):
    keep_ref, *got_refs = refs[:groups]
    total_ref, sum_ref = refs[-2:]
    out_refs = refs[-2 - near : -2]
    piece_refs = refs[groups : -2 - near]
    total = keep_ref[...]
    for ref in got_refs:
        total = total + ref[...].astype(f32)
    total_ref[...] = total
    sum_ref[...] = tree([ref[...].astype(f32) for ref in piece_refs]).astype(bf16)
    place = lax.rem(run_ref[0], near)
    rows = total_ref.shape[0] // near
    below = sum_ref.shape[0] // near
    for k in range(near):
        owner = lax.bitwise_xor(place, k)
        part = total_ref[pl.ds(pl.multiple_of(owner * rows, rows), rows), :].astype(bf16)
        at = 0
        for c in range(0, total_ref.shape[1], lane):
            out_refs[k][at : at + rows, :] = part[:, c : c + lane]
            at += rows
        first = pl.multiple_of(owner * below, 16)
        out_refs[k][at : at + below, :] = sum_ref[pl.ds(first, below), :]


def near_kernel(rows, *refs):
    part = tree([ref[...].astype(f32) for ref in refs[:-2]]).astype(bf16)
    refs[-2][...] = part
    refs[-1][...] = part[rows:, :]


def far_kernel(rows, *refs):
    out_ref = refs[-1]
    out_ref[:rows, :] = tree([ref[:rows, :].astype(f32) for ref in refs[:-1]]).astype(bf16)
    below = refs[0].shape[0] - rows
    for i, ref in enumerate(refs[1:-1]):
        at = rows + i * below
        out_ref[at : at + below, :] = ref[rows:, :]


def gather_kernel(rows, *refs):
    out_ref = refs[-1]
    for i, ref in enumerate(refs[:-1]):
        out_ref[i * rows : (i + 1) * rows, :] = ref[:rows, :]


def spread_rows(chunk_ref, half_ref, near, place):
    rows = half_ref.shape[0] // near
    at = 0
    for m in range(near):
        first = pl.multiple_of(lax.bitwise_xor(place, m) * rows, rows)
        for c in range(0, half_ref.shape[1], lane):
            half_ref[pl.ds(first, rows), c : c + lane] = chunk_ref[at : at + rows, :].astype(f32)
            at += rows


def unpack_kernel(near, far, run_ref, grp_ref, half_in_ref, *refs):
    column_refs = refs[:near]
    side_refs = refs[near : 2 * near]
    cov_hbm, grad_hbm, packed_ref, cov_ref, half_ref, sem = refs[2 * near :]
    chunk = half_ref.shape[0]
    spread_rows(half_in_ref, half_ref, near, lax.rem(run_ref[0], near))
    first = pl.multiple_of(grp_ref[0] * chunk, chunk)
    copies = [
        pltpu.make_async_copy(half_ref, grad_hbm.at[pl.ds(first, chunk), :], sem.at[0])
    ]
    copies[0].start()
    rows = packed_ref.shape[0] // (near * far)
    skip = column_refs[0].shape[0] - (far - 1) * rows
    for m, ref in enumerate(column_refs):
        for k in range(far):
            owner = lax.bitwise_xor(run_ref[0], k * near + m)
            at = skip + (k - 1) * rows
            piece = ref[at : at + rows, :] if k else side_refs[m][...]
            packed_ref[pl.ds(pl.multiple_of(owner * rows, 16), rows), :] = piece
    at = 0
    for i, r in enumerate(range(0, cov_ref.shape[0], lane)):
        for c in range(r, cov_ref.shape[1], lane):
            tile = packed_ref[at : at + lane, :].astype(f32)
            cov_ref[r : r + lane, c : c + lane] = tile
            if c > r:
                cov_ref[c : c + lane, r : r + lane] = tile.T
            at += lane
        copy = pltpu.make_async_copy(
            cov_ref.at[r : r + lane, :], cov_hbm.at[r : r + lane, :], sem.at[i + 1]
        )
        copy.start()
        copies.append(copy)
    for copy in copies:
        copy.wait()


def place_kernel(near, run_ref, grp_ref, *refs):
    grad_hbm, chunk_ref, sem = refs[-3:]
    half_refs = refs[:-4]
    groups = len(half_refs) + 1
    chunk = chunk_ref.shape[1]
    copies = []
    for j, ref in enumerate(half_refs):
        spread_rows(ref, chunk_ref.at[j], near, lax.rem(run_ref[0], near))
        first = pl.multiple_of(lax.rem(grp_ref[0] + j + 1, groups) * chunk, chunk)
        copy = pltpu.make_async_copy(
            chunk_ref.at[j], grad_hbm.at[pl.ds(first, chunk), :], sem.at[j]
        )
        copy.start()
        copies.append(copy)
    for copy in copies:
        copy.wait()


def swap(array, bits, runs):
    return lax.ppermute(array, "blk", [(i, i ^ bits) for i in range(runs)])


def small_call(kernel, shapes, specs, scratch=()):
    vmem = pl.BlockSpec(memory_space=pltpu.VMEM)
    many = isinstance(shapes, tuple)
    return pl.pallas_call(
        kernel,
        out_shape=shapes,
        in_specs=specs,
        out_specs=(vmem,) * len(shapes) if many else vmem,
        scratch_shapes=scratch,
        compiler_params=room(8),
    )


def body(src_feats, tgt_feats, proj_weight, match_blocks, match_count, pair_src, pair_tgt):
    xs = src_feats[0]
    xt = tgt_feats[0]
    points, width = xs.shape
    blocks = pair_src.shape[1]
    block = points // blocks
    runs = lax.axis_size("blk")
    groups = lax.axis_size("grp")
    reach = runs // 16
    run = lax.axis_index("blk")
    grp = lax.axis_index("grp")

    hops = range(1, reach + 1)
    odd = [lax.ppermute(xt, "blk", partners(k, 1, runs)) for k in hops]
    even = [lax.ppermute(xt, "blk", partners(k, 0, runs)) for k in hops]

    tiles = width // lane
    near, far = split(runs)
    piece_rows = -(-tiles * (tiles + 1) // 2 * lane // (16 * runs)) * 16
    column_rows = near * piece_rows
    chunk = width // groups
    grad_rows = chunk // near * tiles
    scale = width / (2.0 * points * runs)
    vmem = pl.BlockSpec(memory_space=pltpu.VMEM)
    smem = pl.BlockSpec(memory_space=pltpu.SMEM)
    hbm = pl.BlockSpec(memory_space=pltpu.HBM)
    run_id = run.reshape(1)
    grp_id = grp.reshape(1)

    far_away = [
        pltpu.with_memory_space_constraint(array, pltpu.HBM)
        for array in (xs, xt, proj_weight, pair_src[0], pair_tgt[0])
    ]
    *pieces, unit, inv, tgt_unit, tgt_inv, sources, targets = pl.pallas_call(
        functools.partial(moment_kernel, far, near, scale),
        out_shape=(jax.ShapeDtypeStruct((column_rows, lane), bf16),) * far
        + (jax.ShapeDtypeStruct((points, width), f32), jax.ShapeDtypeStruct((points, lane), f32))
        * 2
        + (jax.ShapeDtypeStruct(pair_src.shape[1:], jnp.int32),) * 2,
        in_specs=[smem] + [hbm] * 5,
        out_specs=(vmem,) * (far + 6),
        scratch_shapes=[
            pltpu.VMEM((points, width), bf16),
            pltpu.VMEM((points, width), bf16),
            pltpu.VMEM((width, width), bf16),
            pltpu.VMEM((far * column_rows, lane), bf16),
            pltpu.SemaphoreType.DMA((5,)),
        ],
        compiler_params=room(8),
        name="moment",
    )(run_id, *far_away)
    pieces = [pieces[0]] + [swap(pieces[k], k * near, runs) for k in range(1, far)]
    counts, grad, part = pl.pallas_call(
        functools.partial(own_kernel, runs, reach),
        out_shape=(
            jax.ShapeDtypeStruct((points, 2 * reach * points), bf16),
            jax.ShapeDtypeStruct((points, width), f32),
            jax.ShapeDtypeStruct((width, width), f32),
        ),
        in_specs=[smem] * 3 + [vmem] * 6,
        out_specs=(vmem,) * 3,
        scratch_shapes=[pltpu.VMEM((points, (2 * reach + 1) * points + block), f32)],
        compiler_params=room(8 + 4 * reach),
        name="own",
    )(
        run_id, match_blocks[0], match_count, xt, unit, tgt_unit, tgt_inv, sources, targets
    )
    total = [pltpu.VMEM((width, width), f32)]
    send, src_grad, tgt_grad = pl.pallas_call(
        functools.partial(halo_kernel, block, groups),
        out_shape=(
            jax.ShapeDtypeStruct((groups - 1, chunk, width), bf16),
            jax.ShapeDtypeStruct((points, width), bf16),
            jax.ShapeDtypeStruct((2 * reach * points, width), bf16),
        ),
        in_specs=[smem] + [vmem] * (7 + 2 * reach),
        out_specs=(vmem,) * 3,
        scratch_shapes=total,
        compiler_params=room(8 + 4 * reach),
        name="halo",
    )(grp_id, proj_weight, unit, inv, counts, grad, part, xs, *even, *odd)
    got = [
        lax.ppermute(send[k - 1], "grp", [(i, (i + k) % groups) for i in range(groups)])
        for k in range(1, groups)
    ]
    keep = small_call(
        keep_kernel,
        jax.ShapeDtypeStruct((chunk, width), f32),
        [smem] + [vmem] * (4 + 2 * reach),
        total,
    )(grp_id, part, src_grad, tgt_grad, xs, *even, *odd)
    part_shape = jax.ShapeDtypeStruct((grad_rows + piece_rows, lane), bf16)
    parts = small_call(
        functools.partial(deal_kernel, near, groups),
        (part_shape,) * near,
        [smem] + [vmem] * (groups + far),
        [pltpu.VMEM((chunk, width), f32), pltpu.VMEM((column_rows, lane), bf16)],
    )(run_id, keep, *got, *pieces)
    parts = [parts[0]] + [swap(parts[k], k, runs) for k in range(1, near)]
    part, piece = small_call(
        functools.partial(near_kernel, grad_rows),
        (part_shape, jax.ShapeDtypeStruct((piece_rows, lane), bf16)),
        [vmem] * near,
    )(*parts)
    parts = [part] + [swap(part, k * near, runs) for k in range(1, far)]
    sides = [piece] + [swap(piece, k, runs) for k in range(1, near)]
    part = small_call(
        functools.partial(far_kernel, grad_rows),
        jax.ShapeDtypeStruct((grad_rows + (far - 1) * piece_rows, lane), bf16),
        [vmem] * far,
    )(*parts)
    columns = [part] + [swap(part, k, runs) for k in range(1, near)]
    half = small_call(
        functools.partial(gather_kernel, grad_rows),
        jax.ShapeDtypeStruct((near * grad_rows, lane), bf16),
        [vmem] * near,
    )(*columns)
    halves = [half] + [
        lax.ppermute(half, "grp", [(i, (i - k) % groups) for i in range(groups)])
        for k in range(1, groups)
    ]
    square = jax.ShapeDtypeStruct((width, width), f32)
    covariance, own_rows = pl.pallas_call(
        functools.partial(unpack_kernel, near, far),
        out_shape=(square, square),
        in_specs=[smem] * 2 + [vmem] * (1 + 2 * near),
        out_specs=(hbm, hbm),
        scratch_shapes=[
            pltpu.VMEM((far * column_rows, lane), bf16),
            pltpu.VMEM((width, width), f32),
            pltpu.VMEM((chunk, width), f32),
            pltpu.SemaphoreType.DMA((1 + tiles,)),
        ],
        compiler_params=room(8),
        name="unpack",
    )(run_id, grp_id, half, *columns, *sides)
    weight_grad = pl.pallas_call(
        functools.partial(place_kernel, near),
        out_shape=square,
        in_specs=[smem] * 2 + [vmem] * (groups - 1) + [hbm],
        out_specs=hbm,
        scratch_shapes=[
            pltpu.VMEM((groups - 1, chunk, width), f32),
            pltpu.SemaphoreType.DMA((groups - 1,)),
        ],
        input_output_aliases={1 + groups: 0},
        compiler_params=room(8),
        name="place",
    )(run_id, grp_id, *halves[1:], own_rows)
    return (weight_grad, covariance[None])


def solution(mesh):
    placed = (
        P("grp", "blk", None),
        P("grp", "blk", None),
        P(),
        P("grp", "blk", None),
        P("grp", "blk"),
        P("grp", "blk", None, None),
        P("grp", "blk", None, None),
    )
    return jax.shard_map(
        body, mesh=mesh, in_specs=placed, out_specs=(P(), P("grp", None, None)), check_vma=False
    )
```
